32 devices in a mesh: grp: 4 (over x, core), dp: 8 (over z, y).
Axes of the slice: x: 2, y: 2, z: 4, core: 2. Of those that a mesh axis runs over, the one named last changes fastest.
Arguments:
- query: bfloat16 [8, 512, 2560], P('dp', 'grp'), may hold values from -30 to 30
- resp_kv: bfloat16 [8, 512, 1024], P('dp', 'grp'), may hold values from -6 to 6
- prefix_kv: bfloat16 [8, 64, 1024], P('dp', 'grp'), may hold values from -30 to 30
- query_bias: float32 [2560], replicated, may hold values from -3 to 3
- kv_bias: float32 [1024], replicated, may hold values from -3 to 3
- out_grad: bfloat16 [8, 512, 2560], P('dp', 'grp'), may hold values from -6 to 6
- lengths: int32 [8, 4], P('dp', 'grp'), may hold values from 32 to 128
Outputs:
- attended: bfloat16 [8, 512, 2560], P('dp', 'grp')
- query_grad: bfloat16 [8, 512, 2560], P('dp', 'grp')
- resp_kv_grad: bfloat16 [8, 512, 1024], P('dp', 'grp')
- prefix_kv_grad: bfloat16 [8, 64, 1024], P('dp', 'grp')
- query_bias_grad: float32 [2560], replicated
- kv_bias_grad: float32 [1024], replicated
The draws below stay inside these ranges and needn't reach their ends.
All inputs are finite; a program needn't handle non-finite values.
Results may differ from the reference program's by a relative error of at most 0.013.
The reference program's roundings to bfloat16 on the way count: a program that leaves them out, or rounds other values in their place, can miss the bound.
Values may be sent and summed in bfloat16 or wider, within the bound.
A program may use at most 64 MiB of HBM per device.

```python
import jax
import jax.numpy as jnp
from jax import lax

QH = 20
KVH = 4
HD = 128
RESP = 128
PRE = 64
RESP_ALL = 512
PROMPTS = 8
N_GRP = 4


def make_pair(key):
    base = jax.random.fold_in(key, 7)
    first, second = jax.random.split(base, 2)
    queries = jax.random.normal(first, (PROMPTS, RESP_ALL, QH * HD), jnp.float32)
    prefix = jax.random.normal(second, (PROMPTS, PRE, 2 * KVH * HD), jnp.float32)
    return (jnp.clip(queries, -6.0, 6.0), jnp.clip(prefix, -6.0, 6.0))


def draw_query(key, part):
    return make_pair(key)[0].astype(jnp.bfloat16)


def draw_prefix_kv(key, part):
    return make_pair(key)[1].astype(jnp.bfloat16)


def plant(values, rng, low, high):
    place = [jax.random.randint(jax.random.fold_in(rng, axis), (), 0, length) for axis, length in enumerate(values.shape)]
    main_axis = values.shape.index(max(values.shape))
    beside = place[:main_axis] + [(place[main_axis] + 1) % values.shape[main_axis]] + place[main_axis + 1:]
    return values.at[tuple(place)].set(low).at[tuple(beside)].set(high)


def shard_levels(stream_key, extent, cuts, low, top_value):
    gain, own = 1.0, jax.random.fold_in(stream_key, 6)
    for dim, parts in cuts:
        heights = jnp.exp(jax.random.uniform(jax.random.fold_in(own, dim), (parts,), jnp.float32, low / len(cuts), top_value / len(cuts)))
        gain = gain * jnp.repeat(heights, extent[dim] // parts).reshape([-1 if axis == dim else 1 for axis in range(len(extent))])
    return gain


def normal_values(own_key, shape, deviation, limit, cuts=(), kind=jnp.bfloat16):
    entries = jax.random.normal(own_key, shape, jnp.float32) * deviation
    if len(cuts) > 0:
        entries = shard_levels(own_key, shape, cuts, -0.22, 0.18) * entries
    return jnp.clip(entries, min=-limit, max=limit).astype(kind)


def setup_inputs(seed: int = 0) -> dict:
    splits = jax.random.split(jax.random.key(seed), 8)
    return {
        "query": draw_query(jax.random.fold_in(splits[7], 71), 0),
        "resp_kv": normal_values(splits[1], (PROMPTS, RESP_ALL, 2 * KVH * HD), 1.0, 6.0, ((0, 8), (1, 4))),
        "prefix_kv": draw_prefix_kv(jax.random.fold_in(splits[7], 71), 0),
        "query_bias": normal_values(splits[3], (QH * HD,), 0.5, 3.0, (), jnp.float32),
        "kv_bias": normal_values(splits[4], (2 * KVH * HD,), 0.5, 3.0, (), jnp.float32),
        "out_grad": normal_values(splits[5], (PROMPTS, RESP_ALL, QH * HD), 1.0, 6.0, ((0, 8), (1, 4))),
        "lengths": plant(jax.random.randint(splits[6], (PROMPTS, N_GRP), RESP // 4, RESP + 1), jax.random.fold_in(splits[6], 1), RESP // 4, RESP).astype(jnp.int32),
    }


NEG_BIG = -1e30


def attend_group(queries, cotangent, key_blocks, value_blocks, allows):
    factor = queries.shape[-1] ** -0.5
    query_f = queries.astype(jnp.float32)
    grad_f = cotangent.astype(jnp.float32)
    scores = []
    for keys, allow in zip(key_blocks, allows):
        raw = jnp.einsum("thd,sd->hts", query_f, keys.astype(jnp.float32)) * factor
        scores.append(jnp.where(allow[None], raw, NEG_BIG))
    highest = jnp.max(scores[0], -1, keepdims=True)
    for item in scores[1:]:
        highest = jnp.maximum(highest, jnp.max(item, -1, keepdims=True))
    powers = [jnp.exp(item - highest) for item in scores]
    totals = sum(jnp.sum(item, -1, keepdims=True) for item in powers)
    chances = [item / totals for item in powers]
    rounded = [item.astype(jnp.bfloat16) for item in chances]
    output = sum(jnp.einsum("hts,sd->thd", wts.astype(jnp.float32), vals.astype(jnp.float32)) for wts, vals in zip(rounded, value_blocks))
    slopes = [jnp.einsum("thd,sd->hts", grad_f, vals.astype(jnp.float32)) for vals in value_blocks]
    row_dot = sum(jnp.sum(prob * slope, -1, keepdims=True) for prob, slope in zip(chances, slopes))
    shifted = [(prob * (slope - row_dot)).astype(jnp.bfloat16) for prob, slope in zip(chances, slopes)]
    query_grad = sum(jnp.einsum("hts,sd->thd", dsb.astype(jnp.float32), keys.astype(jnp.float32)) for dsb, keys in zip(shifted, key_blocks)) * factor
    key_grads = [jnp.einsum("hts,thd->sd", dsb.astype(jnp.float32), query_f) * factor for dsb in shifted]
    value_grads = [jnp.einsum("hts,thd->sd", wts.astype(jnp.float32), grad_f) for wts in rounded]
    return output, query_grad, key_grads, value_grads


def one_response(query, resp_kv, prefix, cotangent, length, query_bias, kv_bias):
    slots = query.shape[0]
    pre_rows = prefix.shape[0]
    group = QH // KVH
    width = KVH * HD
    biased_query = (query.astype(jnp.float32) + query_bias).astype(jnp.bfloat16)
    own_kv = (resp_kv.astype(jnp.float32) + kv_bias).astype(jnp.bfloat16)
    position = jnp.arange(slots, dtype=jnp.int32)
    live = position < length
    grad_live = jnp.where(live[:, None], cotangent, jnp.zeros_like(cotangent))
    allow_own = position[None, :] <= position[:, None]
    allow_pre = jnp.ones((slots, pre_rows), dtype=bool)
    queries = biased_query.reshape(slots, KVH, group, HD).transpose(1, 0, 2, 3)
    grads = grad_live.reshape(slots, KVH, group, HD).transpose(1, 0, 2, 3)
    pre_keys = prefix[:, :width].reshape(pre_rows, KVH, HD).transpose(1, 0, 2)
    pre_vals = prefix[:, width:].reshape(pre_rows, KVH, HD).transpose(1, 0, 2)
    own_keys = own_kv[:, :width].reshape(slots, KVH, HD).transpose(1, 0, 2)
    own_vals = own_kv[:, width:].reshape(slots, KVH, HD).transpose(1, 0, 2)

    def per_group(pieces):
        qpart, gpart, pkey, pval, okey, oval = pieces
        output, qgrad, kgrads, vgrads = attend_group(qpart, gpart, [pkey, okey], [pval, oval], [allow_pre, allow_own])
        return output, qgrad, kgrads[0], vgrads[0], kgrads[1], vgrads[1]

    output, qgrad, pk_grad, pv_grad, ok_grad, ov_grad = lax.map(per_group, (queries, grads, pre_keys, pre_vals, own_keys, own_vals))
    output = output.transpose(1, 0, 2, 3).reshape(slots, QH * HD)
    attended = jnp.where(live[:, None], output, 0.0).astype(jnp.bfloat16)
    qgrad = qgrad.transpose(1, 0, 2, 3).reshape(slots, QH * HD)
    own_grad = jnp.concatenate([ok_grad.transpose(1, 0, 2).reshape(slots, width), ov_grad.transpose(1, 0, 2).reshape(slots, width)], -1)
    pre_grad = jnp.concatenate([pk_grad.transpose(1, 0, 2).reshape(pre_rows, width), pv_grad.transpose(1, 0, 2).reshape(pre_rows, width)], -1)
    return attended, qgrad, own_grad, pre_grad


def reference(query, resp_kv, prefix_kv, query_bias, kv_bias, out_grad, lengths):
    def prompt(pieces):
        qpart, rpart, ppart, gpart, lpart = pieces
        prefix = (ppart.astype(jnp.float32) + kv_bias).astype(jnp.bfloat16)
        qsplit = qpart.reshape(N_GRP, RESP, QH * HD)
        rsplit = rpart.reshape(N_GRP, RESP, 2 * KVH * HD)
        gsplit = gpart.reshape(N_GRP, RESP, QH * HD)

        def single(qone, rone, gone, lone):
            return one_response(qone, rone, prefix, gone, lone, query_bias, kv_bias)

        attended, qgrad, own_grad, pre_grad = jax.vmap(single)(qsplit, rsplit, gsplit, lpart)
        held = lax.optimization_barrier(pre_grad.astype(jnp.bfloat16))
        pre_sum = jnp.sum(held.astype(jnp.float32), 0).astype(jnp.bfloat16)
        qsum = jnp.sum(qgrad, (0, 1))
        kvsum = jnp.sum(own_grad, (0, 1)) + jnp.sum(pre_grad, (0, 1))
        return (attended.reshape(RESP_ALL, QH * HD), qgrad.astype(jnp.bfloat16).reshape(RESP_ALL, QH * HD),
                own_grad.astype(jnp.bfloat16).reshape(RESP_ALL, 2 * KVH * HD), pre_sum, qsum, kvsum)

    result = lax.map(prompt, (query, resp_kv, prefix_kv, out_grad, lengths))
    return result[0], result[1], result[2], result[3], jnp.sum(result[4], 0), jnp.sum(result[5], 0)
```

```python
import functools

import jax
import jax.numpy as jnp
from jax import lax
from jax.experimental import pallas as pl
from jax.experimental.pallas import tpu as pltpu
from jax.sharding import PartitionSpec as P

QH = 20
KVH = 4
STEP = 2
HD = 128
NEG_BIG = -1e30
TILE = 8
DIRECT = 32
GROUP = QH // KVH
WIDTH = KVH * HD
GCOLS = GROUP * HD
MESH = pl.DeviceIdType.MESH
F32 = jnp.float32
BF16 = jnp.bfloat16

NT = (((1,), (1,)), ((), ()))
NN = (((1,), (0,)), ((), ()))
TN = (((0,), (0,)), ((), ()))


def dot(a, b, dims):
    return lax.dot_general(a, b, dims, preferred_element_type=F32)


def heads_down(x):
    return jnp.concatenate([x[:, h * HD:(h + 1) * HD] for h in range(GROUP)], axis=0)


def kernel(
    n_grp, n_dp, inner,
    len_ref, q_hbm, kv_hbm, pre_hbm, qb_hbm, kvb_hbm, g_hbm,
    att_s, dq_s, dkv_s, dpre_ref, qsum_ref, kvsum_ref,
    pre_ref, qb_ref, kvb_ref, q_s, g_s, kv_s, q2, g2, kv2, sown, dpown, pb_s, ds_s,
    pre_all, pg, pr, b_all, f_all,
    in_sem,
    ag_send, ag_recv, pg_send, pg_recv, b_send, b_recv, f_send, f_recv,
):
    me = lax.axis_index("grp")
    my = lax.axis_index("dp")
    factor = HD ** (-0.5)
    slots = q_s.shape[0]
    own_rows = pre_ref.shape[0]
    pre_rows = n_grp * own_rows
    outer = n_grp // inner
    lane = lax.rem(me, inner)
    row_of = lax.div(me, inner)
    slot = row_of * n_dp + my
    n_slots = outer * n_dp

    across = [(a, b) for b in range(1, n_dp) for a in range(outer)] + [(a, 0) for a in range(1, outer)]

    def at(a, b):
        return {"grp": lax.rem(row_of + a, outer) * inner + lane, "dp": lax.rem(my + b, n_dp)}

    barrier = pltpu.get_barrier_semaphore()
    for off in range(1, n_grp):
        pl.semaphore_signal(barrier, inc=1, device_id={"grp": lax.rem(me + off, n_grp), "dp": my}, device_id_type=MESH)
    far = [at(a, b) for a, b in across if b > 0]
    for peer in far:
        pl.semaphore_signal(barrier, inc=1, device_id=peer, device_id_type=MESH)

    base = 1 + 2 * KVH
    small = [
        pltpu.make_async_copy(src, dst, in_sem.at[base + k])
        for k, (src, dst) in enumerate(
            ((pre_hbm, pre_ref), (kvb_hbm, kvb_ref), (qb_hbm, qb_ref)))
    ]
    loads = [pltpu.make_async_copy(kv_hbm, kv_s, in_sem.at[0])]
    for j in range(KVH):
        cols = pl.ds(j * GCOLS, GCOLS)
        loads.append(pltpu.make_async_copy(q_hbm.at[:, cols], q_s.at[:, cols], in_sem.at[1 + 2 * j]))
        loads.append(pltpu.make_async_copy(g_hbm.at[:, cols], g_s.at[:, cols], in_sem.at[2 + 2 * j]))
    for item in small + loads:
        item.start()
    small[0].wait()
    small[1].wait()
    kvb = kvb_ref[...].reshape(1, 2 * WIDTH)
    mine = (pre_ref[...].astype(F32) + kvb).astype(BF16)
    for j in range(KVH):
        pre_all[j, me] = jnp.concatenate(
            [mine[:, j * HD:(j + 1) * HD], mine[:, WIDTH + j * HD:WIDTH + (j + 1) * HD]], axis=1)

    sent = []

    def exchange(count, here, axis, src, dst, send, recv):
        for off in range(1, count):
            peer = axis(off)
            sent.append(pltpu.make_async_remote_copy(
                src_ref=src(peer["grp"]), dst_ref=dst.at[here],
                send_sem=send.at[off - 1], recv_sem=recv.at[here],
                device_id=peer, device_id_type=MESH))
            sent[-1].start()

    def arrived(count, here, axis, src, dst, send, recv):
        for off in range(1, count):
            peer = axis(off)
            there = lax.rem(here + off, count)
            pltpu.make_async_remote_copy(
                src_ref=src(peer["grp"]), dst_ref=dst.at[there],
                send_sem=send.at[off - 1], recv_sem=recv.at[there],
                device_id=peer, device_id_type=MESH).wait_recv()

    def group(off):
        return {"grp": lax.rem(me + off, n_grp), "dp": my}

    def part(off):
        return {"grp": row_of * inner + lax.rem(lane + off, inner), "dp": my}

    ag = [(n_grp, me, group, lambda peer, j=j: pre_all.at[j, me], pre_all.at[j], ag_send.at[j], ag_recv.at[j])
          for j in range(KVH)]
    rs = [(n_grp, me, group, lambda peer, j=j: pg.at[j, peer], pr.at[j], pg_send.at[j], pg_recv.at[j])
          for j in range(KVH)]
    last = (inner, lane, part, lambda peer: f_all.at[lane], f_all, f_send, f_recv)

    pl.semaphore_wait(barrier, n_grp - 1 + len(far))
    for j in range(KVH):
        exchange(*ag[j])

    length = len_ref[0, 0]
    live_in = lax.broadcasted_iota(jnp.int32, (slots, GCOLS), 0) < length
    live_out = lax.broadcasted_iota(jnp.int32, (slots, HD), 0) < length
    key_at = lax.broadcasted_iota(jnp.int32, (slots, slots), 0)
    row_at = lax.broadcasted_iota(jnp.int32, (slots, slots), 1)
    allow = jnp.concatenate([key_at <= row_at] * GROUP, axis=1)
    head_row = lax.broadcasted_iota(jnp.int32, (TILE, slots), 0)
    pick = jnp.concatenate([(head_row == h).astype(F32).astype(BF16) for h in range(GROUP)], axis=1)
    bias_row = lax.broadcasted_iota(jnp.int32, (TILE, HD), 0)

    loads[0].wait()
    small[2].wait()
    kv2[...] = (kv_s[...].astype(F32) + kvb).astype(BF16)
    qb = qb_ref[...].reshape(1, QH * HD)
    def ready(j):
        cols = slice(j * GCOLS, (j + 1) * GCOLS)
        loads[1 + 2 * j].wait()
        loads[2 + 2 * j].wait()
        qj = heads_down((q_s[:, cols].astype(F32) + qb[:, cols]).astype(BF16))
        gj = g_s[:, cols]
        gj = heads_down(jnp.where(live_in, gj, jnp.zeros_like(gj)))
        q2[j] = qj
        g2[j] = gj
        raw = dot(kv2[:, j * HD:(j + 1) * HD], qj, NT) * factor
        sown[j] = jnp.where(allow, raw, NEG_BIG)
        dpown[j] = dot(kv2[:, WIDTH + j * HD:WIDTH + (j + 1) * HD], gj, NT)

    for j in range(KVH):
        ready(j)

    def keys_of(j):
        both = pre_all[j].reshape(pre_rows, 2 * HD)
        return jnp.concatenate([both[:, :HD], kv2[:, j * HD:(j + 1) * HD]], axis=0)

    rows = []
    for j in range(KVH):
        if j % STEP == 0:
            for k in range(j, j + STEP):
                arrived(*ag[k])
        kc = slice(j * HD, (j + 1) * HD)
        vc = slice(WIDTH + j * HD, WIDTH + (j + 1) * HD)
        both = pre_all[j].reshape(pre_rows, 2 * HD)
        pk = both[:, :HD]
        pv = both[:, HD:]
        qj = q2[j]
        gj = g2[j]
        s_p = dot(pk, qj, NT) * factor
        s_o = sown[j]
        dp_p = dot(pv, gj, NT)
        dp_o = dpown[j]
        top = jnp.maximum(jnp.max(s_p, 0, keepdims=True), jnp.max(s_o, 0, keepdims=True))
        e_p = jnp.exp(s_p - top)
        e_o = jnp.exp(s_o - top)
        inv = 1.0 / (jnp.sum(e_p, 0, keepdims=True) + jnp.sum(e_o, 0, keepdims=True))
        p_p = e_p * inv
        p_o = e_o * inv
        row = jnp.sum(p_p * dp_p, 0, keepdims=True) + jnp.sum(p_o * dp_o, 0, keepdims=True)
        ds = jnp.concatenate([(p_p * (dp_p - row)).astype(BF16), (p_o * (dp_o - row)).astype(BF16)], axis=0)
        pb = jnp.concatenate([p_p.astype(BF16), p_o.astype(BF16)], axis=0)
        pb_s[j] = pb
        ds_s[j] = ds
        heads = dot(pick, ds, NT)
        high = heads.astype(BF16)
        low = (heads - high.astype(F32)).astype(BF16)
        split = dot(jnp.concatenate([high, low], axis=0), keys_of(j), NN) * factor
        dk = dot(ds, qj, NN) * factor
        dv = dot(pb, gj, NN)
        dkr = dk.astype(BF16)
        dvr = dv.astype(BF16)
        pg[j] = jnp.concatenate([dkr[:pre_rows], dvr[:pre_rows]], axis=1).reshape(n_grp, own_rows, 2 * HD)
        dkv_s[:, kc] = dkr[pre_rows:]
        dkv_s[:, vc] = dvr[pre_rows:]
        block = split[:TILE] + split[TILE:]
        block = jnp.where(bias_row == GROUP, jnp.sum(dk, 0, keepdims=True), block)
        rows.append(jnp.where(bias_row == GROUP + 1, jnp.sum(dv, 0, keepdims=True), block))
        if j % STEP == STEP - 1:
            c = j // STEP
            b_all[c, slot] = jnp.concatenate(rows, axis=0).astype(BF16)
            rows = []
            for k, (a, b) in enumerate(across):
                sent.append(pltpu.make_async_remote_copy(
                    src_ref=b_all.at[c, slot], dst_ref=b_all.at[c, slot],
                    send_sem=b_send.at[c, k], recv_sem=b_recv.at[c, slot],
                    device_id=at(a, b), device_id_type=MESH))
                sent[-1].start()
    for j in range(KVH):
        exchange(*rs[j])

    for j in range(KVH):
        dq = dot(ds_s[j], keys_of(j), TN) * factor
        pv = pre_all[j].reshape(pre_rows, 2 * HD)[:, HD:]
        vals = jnp.concatenate([pv, kv2[:, WIDTH + j * HD:WIDTH + (j + 1) * HD]], axis=0)
        out = dot(pb_s[j], vals, TN)
        for h in range(GROUP):
            here = slice((j * GROUP + h) * HD, (j * GROUP + h + 1) * HD)
            dq_s[:, here] = dq[h * slots:(h + 1) * slots].astype(BF16)
            att_s[:, here] = jnp.where(live_out, out[h * slots:(h + 1) * slots], 0.0).astype(BF16)

    for j in range(KVH):
        arrived(*rs[j])
        pr[j, me] = pg[j, me]
        acc = pr[j, 0].astype(F32)
        for k in range(1, n_grp):
            acc = acc + pr[j, k].astype(F32)
        acc = acc.astype(BF16)
        dpre_ref[:, j * HD:(j + 1) * HD] = acc[:, :HD]
        dpre_ref[:, WIDTH + j * HD:WIDTH + (j + 1) * HD] = acc[:, HD:]

    for c in range(KVH // STEP):
        for k, (a, b) in enumerate(across):
            there = lax.rem(row_of + a, outer) * n_dp + lax.rem(my + b, n_dp)
            pltpu.make_async_remote_copy(
                src_ref=b_all.at[c, slot], dst_ref=b_all.at[c, there],
                send_sem=b_send.at[c, k], recv_sem=b_recv.at[c, there],
                device_id=at(a, b), device_id_type=MESH).wait_recv()
        total = b_all[c, 0].astype(F32)
        for k in range(1, n_slots):
            total = total + b_all[c, k].astype(F32)
        f_all[lane, c] = total
    exchange(*last)
    for item in sent:
        item.wait_send()
    arrived(*last)
    for c in range(KVH // STEP):
        total = f_all[0, c]
        for k in range(1, inner):
            total = total + f_all[k, c]
        for k in range(STEP):
            j = c * STEP + k
            for h in range(GROUP):
                qsum_ref[pl.ds((j * GROUP + h) * HD, HD)] = total[k * TILE + h]
            kvsum_ref[pl.ds(j * HD, HD)] = total[k * TILE + GROUP]
            kvsum_ref[pl.ds(WIDTH + j * HD, HD)] = total[k * TILE + GROUP + 1]


def write_out(*refs):
    count = (len(refs) - 1) // 2
    copies = [pltpu.make_async_copy(refs[k], refs[count + k], refs[-1].at[k]) for k in range(count)]
    for item in copies:
        item.start()
    for item in copies:
        item.wait()


def local(n_grp, n_dp, query, resp_kv, prefix_kv, query_bias, kv_bias, out_grad, lengths):
    slots = query.shape[1]
    own_rows = prefix_kv.shape[1]
    pre_rows = own_rows * n_grp
    inner = 2 if n_grp % 2 == 0 and n_grp // 2 * n_dp <= DIRECT else n_grp
    n_slots = n_grp // inner * n_dp
    chunks = KVH // STEP
    qw = QH * HD
    kw = 2 * WIDTH
    hbm = pl.BlockSpec(memory_space=pltpu.HBM)
    vmem = pl.BlockSpec(memory_space=pltpu.VMEM)
    dma = lambda *n: pltpu.SemaphoreType.DMA(n)
    shapes = (
        jax.ShapeDtypeStruct((slots, qw), BF16),
        jax.ShapeDtypeStruct((slots, qw), BF16),
        jax.ShapeDtypeStruct((slots, kw), BF16),
        jax.ShapeDtypeStruct((own_rows, kw), BF16),
        jax.ShapeDtypeStruct((qw,), F32),
        jax.ShapeDtypeStruct((kw,), F32),
    )
    outs = pl.pallas_call(
        functools.partial(kernel, n_grp, n_dp, inner),
        name="replay",
        out_shape=shapes,
        in_specs=[pl.BlockSpec(memory_space=pltpu.SMEM)] + [hbm] * 6,
        out_specs=(vmem,) * 6,
        scratch_shapes=[
            pltpu.VMEM((own_rows, kw), BF16),
            pltpu.VMEM((qw,), F32),
            pltpu.VMEM((kw,), F32),
            pltpu.VMEM((slots, qw), BF16),
            pltpu.VMEM((slots, qw), BF16),
            pltpu.VMEM((slots, kw), BF16),
            pltpu.VMEM((KVH, GROUP * slots, HD), BF16),
            pltpu.VMEM((KVH, GROUP * slots, HD), BF16),
            pltpu.VMEM((slots, kw), BF16),
            pltpu.VMEM((KVH, slots, GROUP * slots), F32),
            pltpu.VMEM((KVH, slots, GROUP * slots), F32),
            pltpu.VMEM((KVH, pre_rows + slots, GROUP * slots), BF16),
            pltpu.VMEM((KVH, pre_rows + slots, GROUP * slots), BF16),
            pltpu.VMEM((KVH, n_grp, own_rows, 2 * HD), BF16),
            pltpu.VMEM((KVH, n_grp, own_rows, 2 * HD), BF16),
            pltpu.VMEM((KVH, n_grp, own_rows, 2 * HD), BF16),
            pltpu.VMEM((chunks, n_slots, STEP * TILE, HD), BF16),
            pltpu.VMEM((inner, chunks, STEP * TILE, HD), F32),
            dma(4 + 2 * KVH),
            dma(KVH, n_grp - 1), dma(KVH, n_grp), dma(KVH, n_grp - 1), dma(KVH, n_grp),
            dma(chunks, n_slots - 1), dma(chunks, n_slots),
            dma(inner - 1), dma(inner),
        ],
        compiler_params=pltpu.CompilerParams(
            collective_id=0, has_side_effects=True, vmem_limit_bytes=24 * 1024 * 1024
        ),
    )(lengths, *(pltpu.with_memory_space_constraint(x, pltpu.HBM) for x in (query[0], resp_kv[0], prefix_kv[0], query_bias, kv_bias, out_grad[0])))
    att, dq, dkv, dpre, qsum, kvsum = pl.pallas_call(
        write_out,
        name="write_out",
        out_shape=shapes,
        in_specs=[vmem] * 6,
        out_specs=(hbm,) * 6,
        scratch_shapes=[dma(6)],
        compiler_params=pltpu.CompilerParams(vmem_limit_bytes=1024 * 1024),
    )(*outs)
    return att[None], dq[None], dkv[None], dpre[None], qsum, kvsum


def solution(mesh):
    return jax.shard_map(
        functools.partial(local, mesh.shape["grp"], mesh.shape["dp"]),
        mesh=mesh,
        in_specs=(
            P("dp", "grp", None),
            P("dp", "grp", None),
            P("dp", "grp", None),
            P(),
            P(),
            P("dp", "grp", None),
            P("dp", "grp"),
        ),
        out_specs=(
            P("dp", "grp", None),
            P("dp", "grp", None),
            P("dp", "grp", None),
            P("dp", "grp", None),
            P(),
            P(),
        ),
        check_vma=False,
    )
```

```python
import functools

import jax
import jax.numpy as jnp
from jax import lax
from jax.experimental import pallas as pl
from jax.experimental.pallas import tpu as pltpu
from jax.sharding import PartitionSpec as P

QH = 20
KVH = 4
STEP = 2
HD = 128
NEG_BIG = -1e30
TILE = 8
DIRECT = 32
GROUP = QH // KVH
WIDTH = KVH * HD
GCOLS = GROUP * HD
MESH = pl.DeviceIdType.MESH
F32 = jnp.float32
BF16 = jnp.bfloat16

NT = (((1,), (1,)), ((), ()))
NN = (((1,), (0,)), ((), ()))
TN = (((0,), (0,)), ((), ()))


def dot(a, b, dims):
    return lax.dot_general(a, b, dims, preferred_element_type=F32)


def heads_down(x):
    return jnp.concatenate([x[:, h * HD:(h + 1) * HD] for h in range(GROUP)], axis=0)


def kernel(
    n_grp, n_dp, inner,
    len_ref, q_hbm, kv_hbm, pre_hbm, qb_hbm, kvb_hbm, g_hbm,
    att_s, dq_s, dkv_s, dpre_ref, qsum_ref, kvsum_ref,
    pre_ref, qb_ref, kvb_ref, q_s, g_s, kv_s, q2, g2, kv2, eown, dpown, stat, pb_s, ds_s,
    pre_all, pg, pr, b_all, f_all,
    in_sem, ag_sem, rs_sem, b_sem, f_sem,
):
    me = lax.axis_index("grp")
    my = lax.axis_index("dp")
    factor = HD ** (-0.5)
    slots = q_s.shape[0]
    own_rows = pre_ref.shape[0]
    pre_rows = n_grp * own_rows
    outer = n_grp // inner
    lane = lax.rem(me, inner)
    row_of = lax.div(me, inner)
    slot = row_of * n_dp + my
    n_slots = outer * n_dp

    across = [(a, b) for b in range(1, n_dp) for a in range(outer)] + [(a, 0) for a in range(1, outer)]

    def at(a, b):
        return {"grp": lax.rem(row_of + a, outer) * inner + lane, "dp": lax.rem(my + b, n_dp)}

    def group(off):
        return {"grp": lax.rem(me + off, n_grp), "dp": my}

    def part(off):
        return {"grp": row_of * inner + lax.rem(lane + off, inner), "dp": my}

    loads = [
        pltpu.make_async_copy(src, dst, in_sem.at[k])
        for k, (src, dst) in enumerate((
            (pre_hbm, pre_ref), (kvb_hbm, kvb_ref), (qb_hbm, qb_ref), (kv_hbm, kv_s), (q_hbm, q_s), (g_hbm, g_s)))
    ]
    for item in loads[:2]:
        item.start()
    barrier = pltpu.get_barrier_semaphore()
    for off in range(1, n_grp):
        pl.semaphore_signal(barrier, inc=1, device_id=group(off), device_id_type=MESH)
    far = [at(a, b) for a, b in across if b > 0]
    for peer in far:
        pl.semaphore_signal(barrier, inc=1, device_id=peer, device_id_type=MESH)
    for item in loads[2:]:
        item.start()

    loads[0].wait()
    loads[1].wait()
    kvb = kvb_ref[...].reshape(1, 2 * WIDTH)
    mine = (pre_ref[...].astype(F32) + kvb).astype(BF16)
    for j in range(KVH):
        pre_all[j // STEP, me, :, (j % STEP) * 2 * HD:(j % STEP + 1) * 2 * HD] = jnp.concatenate(
            [mine[:, j * HD:(j + 1) * HD], mine[:, WIDTH + j * HD:WIDTH + (j + 1) * HD]], axis=1)

    def send(src, dst, sems, recv, peer):
        pltpu.make_async_remote_copy(
            src_ref=src, dst_ref=dst, send_sem=sems.at[0], recv_sem=sems.at[recv],
            device_id=peer, device_id_type=MESH).start()

    def take(like, sem):
        pltpu.make_async_copy(like, like, sem).wait()

    pl.semaphore_wait(barrier, n_grp - 1 + len(far))
    for c in range(KVH // STEP):
        for off in range(1, n_grp):
            send(pre_all.at[c, me], pre_all.at[c, me], ag_sem, 1 + c, group(off))

    length = len_ref[0, 0]
    live_in = lax.broadcasted_iota(jnp.int32, (slots, GCOLS), 0) < length
    live_out = lax.broadcasted_iota(jnp.int32, (slots, HD), 0) < length
    key_at = lax.broadcasted_iota(jnp.int32, (slots, slots), 0)
    row_at = lax.broadcasted_iota(jnp.int32, (slots, slots), 1)
    allow = jnp.concatenate([key_at <= row_at] * GROUP, axis=1)
    pick = (lax.broadcasted_iota(jnp.int32, (GROUP * slots, HD), 1)
            == lax.div(lax.broadcasted_iota(jnp.int32, (GROUP * slots, HD), 0), slots)).astype(F32).astype(BF16)
    bias_row = lax.broadcasted_iota(jnp.int32, (TILE, HD), 0)

    for item in loads[2:]:
        item.wait()
    kv2[...] = (kv_s[...].astype(F32) + kvb).astype(BF16)
    qb = qb_ref[...].reshape(1, QH * HD)
    def ready(j):
        cols = slice(j * GCOLS, (j + 1) * GCOLS)
        qj = heads_down((q_s[:, cols].astype(F32) + qb[:, cols]).astype(BF16))
        gj = g_s[:, cols]
        gj = heads_down(jnp.where(live_in, gj, jnp.zeros_like(gj)))
        q2[j] = qj
        g2[j] = gj
        raw = dot(kv2[:, j * HD:(j + 1) * HD], qj, NT) * factor
        raw = jnp.where(allow, raw, NEG_BIG)
        dpo = dot(kv2[:, WIDTH + j * HD:WIDTH + (j + 1) * HD], gj, NT)
        top = jnp.max(raw, 0, keepdims=True)
        e = jnp.exp(raw - top)
        eown[j] = e
        dpown[j] = dpo
        stat[j, 0:1] = top
        stat[j, 1:2] = jnp.sum(e, 0, keepdims=True)
        stat[j, 2:3] = jnp.sum(e * dpo, 0, keepdims=True)

    for j in range(KVH):
        ready(j)

    def prompt(j):
        both = pre_all[j // STEP, :, :, (j % STEP) * 2 * HD:(j % STEP + 1) * 2 * HD].reshape(pre_rows, 2 * HD)
        return both[:, :HD], both[:, HD:]

    def keys_of(j):
        return jnp.concatenate([prompt(j)[0], kv2[:, j * HD:(j + 1) * HD]], axis=0)

    rows = []
    for j in range(KVH):
        if j % STEP == 0:
            take(pre_all.at[j // STEP, pl.ds(0, n_grp - 1)], ag_sem.at[1 + j // STEP])
        kc = slice(j * HD, (j + 1) * HD)
        vc = slice(WIDTH + j * HD, WIDTH + (j + 1) * HD)
        pk, pv = prompt(j)
        qj = q2[j]
        gj = g2[j]
        s_p = dot(pk, qj, NT) * factor
        dp_p = dot(pv, gj, NT)
        top_o = stat[j, 0:1]
        top = jnp.maximum(jnp.max(s_p, 0, keepdims=True), top_o)
        e_p = jnp.exp(s_p - top)
        shift = jnp.exp(top_o - top)
        inv = 1.0 / (jnp.sum(e_p, 0, keepdims=True) + shift * stat[j, 1:2])
        scale = shift * inv
        p_p = e_p * inv
        p_o = eown[j] * scale
        dp_o = dpown[j]
        row = jnp.sum(p_p * dp_p, 0, keepdims=True) + scale * stat[j, 2:3]
        ds = jnp.concatenate([(p_p * (dp_p - row)).astype(BF16), (p_o * (dp_o - row)).astype(BF16)], axis=0)
        pb = jnp.concatenate([p_p.astype(BF16), p_o.astype(BF16)], axis=0)
        pb_s[j] = pb
        ds_s[j] = ds
        both = dot(ds, jnp.concatenate([qj, pick], axis=1), NN)
        dk = both[:, :HD] * factor
        heads = jnp.transpose(both[:, HD:])[:TILE]
        high = heads.astype(BF16).astype(F32)
        split = dot(jnp.concatenate([high, heads - high], axis=0).astype(BF16), keys_of(j), NN) * factor
        dv = dot(pb, gj, NN)
        dkr = dk.astype(BF16)
        dvr = dv.astype(BF16)
        pg[:, :, kc] = dkr[:pre_rows].reshape(n_grp, own_rows, HD)
        pg[:, :, vc] = dvr[:pre_rows].reshape(n_grp, own_rows, HD)
        dkv_s[:, kc] = dkr[pre_rows:]
        dkv_s[:, vc] = dvr[pre_rows:]
        block = split[:TILE] + split[TILE:]
        block = jnp.where(bias_row == GROUP, jnp.sum(dk, 0, keepdims=True), block)
        rows.append(jnp.where(bias_row == GROUP + 1, jnp.sum(dv, 0, keepdims=True), block))
        if j % STEP == STEP - 1:
            c = j // STEP
            b_all[c, slot] = jnp.concatenate(rows, axis=0).astype(BF16)
            rows = []
            for a, b in across:
                send(b_all.at[c, slot], b_all.at[c, slot], b_sem, 1 + c, at(a, b))
    for off in range(1, n_grp):
        peer = group(off)
        send(pg.at[peer["grp"]], pr.at[me], rs_sem, 1, peer)

    for j in range(KVH):
        dq = dot(ds_s[j], keys_of(j), TN) * factor
        vals = jnp.concatenate([prompt(j)[1], kv2[:, WIDTH + j * HD:WIDTH + (j + 1) * HD]], axis=0)
        out = dot(pb_s[j], vals, TN)
        for h in range(GROUP):
            here = slice((j * GROUP + h) * HD, (j * GROUP + h + 1) * HD)
            dq_s[:, here] = dq[h * slots:(h + 1) * slots].astype(BF16)
            att_s[:, here] = jnp.where(live_out, out[h * slots:(h + 1) * slots], 0.0).astype(BF16)

    take(pr.at[pl.ds(0, n_grp - 1)], rs_sem.at[1])
    pr[me] = pg[me]
    acc = pr[0].astype(F32)
    for k in range(1, n_grp):
        acc = acc + pr[k].astype(F32)
    dpre_ref[...] = acc.astype(BF16)

    for c in range(KVH // STEP):
        take(b_all.at[c, pl.ds(0, n_slots - 1)], b_sem.at[1 + c])
        total = b_all[c, 0].astype(F32)
        for k in range(1, n_slots):
            total = total + b_all[c, k].astype(F32)
        f_all[lane, c] = total
    for off in range(1, inner):
        send(f_all.at[lane], f_all.at[lane], f_sem, 1, part(off))
    take(pre_all.at[:, pl.ds(0, n_grp - 1)], ag_sem.at[0])
    take(pr.at[pl.ds(0, n_grp - 1)], rs_sem.at[0])
    take(b_all.at[:, pl.ds(0, n_slots - 1)], b_sem.at[0])
    take(f_all.at[pl.ds(0, inner - 1)], f_sem.at[0])
    take(f_all.at[pl.ds(0, inner - 1)], f_sem.at[1])
    for c in range(KVH // STEP):
        total = f_all[0, c]
        for k in range(1, inner):
            total = total + f_all[k, c]
        for k in range(STEP):
            j = c * STEP + k
            for h in range(GROUP):
                qsum_ref[pl.ds((j * GROUP + h) * HD, HD)] = total[k * TILE + h]
            kvsum_ref[pl.ds(j * HD, HD)] = total[k * TILE + GROUP]
            kvsum_ref[pl.ds(WIDTH + j * HD, HD)] = total[k * TILE + GROUP + 1]


def write_out(*refs):
    count = (len(refs) - 1) // 2
    copies = [pltpu.make_async_copy(refs[k], refs[count + k], refs[-1].at[k]) for k in range(count)]
    for item in copies:
        item.start()
    for item in copies:
        item.wait()


def local(n_grp, n_dp, query, resp_kv, prefix_kv, query_bias, kv_bias, out_grad, lengths):
    slots = query.shape[1]
    own_rows = prefix_kv.shape[1]
    pre_rows = own_rows * n_grp
    inner = 2 if n_grp % 2 == 0 and n_grp // 2 * n_dp <= DIRECT else n_grp
    n_slots = n_grp // inner * n_dp
    chunks = KVH // STEP
    qw = QH * HD
    kw = 2 * WIDTH
    hbm = pl.BlockSpec(memory_space=pltpu.HBM)
    vmem = pl.BlockSpec(memory_space=pltpu.VMEM)
    dma = lambda *n: pltpu.SemaphoreType.DMA(n)
    shapes = (
        jax.ShapeDtypeStruct((slots, qw), BF16),
        jax.ShapeDtypeStruct((slots, qw), BF16),
        jax.ShapeDtypeStruct((slots, kw), BF16),
        jax.ShapeDtypeStruct((own_rows, kw), BF16),
        jax.ShapeDtypeStruct((qw,), F32),
        jax.ShapeDtypeStruct((kw,), F32),
    )
    outs = pl.pallas_call(
        functools.partial(kernel, n_grp, n_dp, inner),
        name="replay",
        out_shape=shapes,
        in_specs=[pl.BlockSpec(memory_space=pltpu.SMEM)] + [hbm] * 6,
        out_specs=(vmem,) * 6,
        scratch_shapes=[
            pltpu.VMEM((own_rows, kw), BF16),
            pltpu.VMEM((qw,), F32),
            pltpu.VMEM((kw,), F32),
            pltpu.VMEM((slots, qw), BF16),
            pltpu.VMEM((slots, qw), BF16),
            pltpu.VMEM((slots, kw), BF16),
            pltpu.VMEM((KVH, GROUP * slots, HD), BF16),
            pltpu.VMEM((KVH, GROUP * slots, HD), BF16),
            pltpu.VMEM((slots, kw), BF16),
            pltpu.VMEM((KVH, slots, GROUP * slots), F32),
            pltpu.VMEM((KVH, slots, GROUP * slots), F32),
            pltpu.VMEM((KVH, TILE, GROUP * slots), F32),
            pltpu.VMEM((KVH, pre_rows + slots, GROUP * slots), BF16),
            pltpu.VMEM((KVH, pre_rows + slots, GROUP * slots), BF16),
            pltpu.VMEM((chunks, n_grp, own_rows, STEP * 2 * HD), BF16),
            pltpu.VMEM((n_grp, own_rows, kw), BF16),
            pltpu.VMEM((n_grp, own_rows, kw), BF16),
            pltpu.VMEM((chunks, n_slots, STEP * TILE, HD), BF16),
            pltpu.VMEM((inner, chunks, STEP * TILE, HD), F32),
            dma(6), dma(1 + chunks), dma(2), dma(1 + chunks), dma(2),
        ],
        compiler_params=pltpu.CompilerParams(
            collective_id=0, has_side_effects=True, vmem_limit_bytes=24 * 1024 * 1024
        ),
    )(lengths, *(pltpu.with_memory_space_constraint(x, pltpu.HBM) for x in (query[0], resp_kv[0], prefix_kv[0], query_bias, kv_bias, out_grad[0])))
    att, dq, dkv, dpre, qsum, kvsum = pl.pallas_call(
        write_out,
        name="write_out",
        out_shape=shapes,
        in_specs=[vmem] * 6,
        out_specs=(hbm,) * 6,
        scratch_shapes=[dma(6)],
        compiler_params=pltpu.CompilerParams(vmem_limit_bytes=1024 * 1024),
    )(*outs)
    return att[None], dq[None], dkv[None], dpre[None], qsum, kvsum


def solution(mesh):
    return jax.shard_map(
        functools.partial(local, mesh.shape["grp"], mesh.shape["dp"]),
        mesh=mesh,
        in_specs=(
            P("dp", "grp", None),
            P("dp", "grp", None),
            P("dp", "grp", None),
            P(),
            P(),
            P("dp", "grp", None),
            P("dp", "grp"),
        ),
        out_specs=(
            P("dp", "grp", None),
            P("dp", "grp", None),
            P("dp", "grp", None),
            P("dp", "grp", None),
            P(),
            P(),
        ),
        check_vma=False,
    )
```

```python
import functools

import jax
import jax.numpy as jnp
from jax import lax
from jax.experimental import pallas as pl
from jax.experimental.pallas import tpu as pltpu
from jax.sharding import PartitionSpec as P

QH = 20
KVH = 4
STEP = 2
HD = 128
NEG_BIG = -1e30
TILE = 8
DIRECT = 32
GROUP = QH // KVH
WIDTH = KVH * HD
GCOLS = GROUP * HD
MESH = pl.DeviceIdType.MESH
F32 = jnp.float32
BF16 = jnp.bfloat16

NT = (((1,), (1,)), ((), ()))
NN = (((1,), (0,)), ((), ()))
TN = (((0,), (0,)), ((), ()))


def dot(a, b, dims):
    return lax.dot_general(a, b, dims, preferred_element_type=F32)


def heads_down(x):
    return jnp.concatenate([x[:, h * HD:(h + 1) * HD] for h in range(GROUP)], axis=0)


def kernel(
    n_grp, n_dp, inner,
    len_ref, q_hbm, kv_hbm, pre_hbm, qb_hbm, kvb_hbm, g_hbm,
    att_s, dq_s, dkv_s, dpre_ref, qsum_ref, kvsum_ref,
    pre_ref, qb_ref, kvb_ref, q_s, g_s, kv_s, q2, g2, kv2, eown, dpown, stat, gsum, pb_s, ds_s,
    pre_all, pg, pr, b_all, f_all,
    in_sem, ag_sem, rs_sem, b_sem, f_sem,
):
    me = lax.axis_index("grp")
    my = lax.axis_index("dp")
    factor = HD ** (-0.5)
    slots = q_s.shape[0]
    own_rows = pre_ref.shape[0]
    pre_rows = n_grp * own_rows
    outer = n_grp // inner
    lane = lax.rem(me, inner)
    row_of = lax.div(me, inner)
    slot = row_of * n_dp + my
    n_slots = outer * n_dp

    across = [(a, b) for b in range(1, n_dp) for a in range(outer)] + [(a, 0) for a in range(1, outer)]

    def at(a, b):
        return {"grp": lax.rem(row_of + a, outer) * inner + lane, "dp": lax.rem(my + b, n_dp)}

    def group(off):
        return {"grp": lax.rem(me + off, n_grp), "dp": my}

    def part(off):
        return {"grp": row_of * inner + lax.rem(lane + off, inner), "dp": my}

    loads = [
        pltpu.make_async_copy(src, dst, in_sem.at[k])
        for k, (src, dst) in enumerate((
            (pre_hbm, pre_ref), (kvb_hbm, kvb_ref), (qb_hbm, qb_ref), (kv_hbm, kv_s), (q_hbm, q_s), (g_hbm, g_s)))
    ]
    for item in loads[:2]:
        item.start()
    barrier = pltpu.get_barrier_semaphore()
    for off in range(1, n_grp):
        pl.semaphore_signal(barrier, inc=1, device_id=group(off), device_id_type=MESH)
    far = [at(a, b) for a, b in across if b > 0]
    for peer in far:
        pl.semaphore_signal(barrier, inc=1, device_id=peer, device_id_type=MESH)
    for item in loads[2:]:
        item.start()

    loads[0].wait()
    loads[1].wait()
    kvb = kvb_ref[...].reshape(1, 2 * WIDTH)
    mine = (pre_ref[...].astype(F32) + kvb).astype(BF16)
    for j in range(KVH):
        pre_all[j // STEP, me, :, (j % STEP) * 2 * HD:(j % STEP + 1) * 2 * HD] = jnp.concatenate(
            [mine[:, j * HD:(j + 1) * HD], mine[:, WIDTH + j * HD:WIDTH + (j + 1) * HD]], axis=1)

    def send(src, dst, sems, recv, peer):
        pltpu.make_async_remote_copy(
            src_ref=src, dst_ref=dst, send_sem=sems.at[0], recv_sem=sems.at[recv],
            device_id=peer, device_id_type=MESH).start()

    def take(like, sem):
        pltpu.make_async_copy(like, like, sem).wait()

    pl.semaphore_wait(barrier, n_grp - 1 + len(far))
    for c in range(KVH // STEP):
        for off in range(1, n_grp):
            send(pre_all.at[c, me], pre_all.at[c, me], ag_sem, 1 + c, group(off))

    length = len_ref[0, 0]
    live_in = lax.broadcasted_iota(jnp.int32, (slots, GCOLS), 0) < length
    live_out = lax.broadcasted_iota(jnp.int32, (slots, HD), 0) < length
    key_at = lax.broadcasted_iota(jnp.int32, (slots, slots), 0)
    row_at = lax.broadcasted_iota(jnp.int32, (slots, slots), 1)
    allow = jnp.concatenate([key_at <= row_at] * GROUP, axis=1)
    pick = (lax.broadcasted_iota(jnp.int32, (GROUP * slots, HD), 1)
            == lax.div(lax.broadcasted_iota(jnp.int32, (GROUP * slots, HD), 0), slots)).astype(F32).astype(BF16)
    bias_row = lax.broadcasted_iota(jnp.int32, (TILE, HD), 0)

    for item in loads[2:]:
        item.wait()
    kv2[...] = (kv_s[...].astype(F32) + kvb).astype(BF16)
    qb = qb_ref[...].reshape(1, QH * HD)
    def ready(j):
        cols = slice(j * GCOLS, (j + 1) * GCOLS)
        qj = heads_down((q_s[:, cols].astype(F32) + qb[:, cols]).astype(BF16))
        gj = g_s[:, cols]
        gj = heads_down(jnp.where(live_in, gj, jnp.zeros_like(gj)))
        q2[j] = qj
        g2[j] = gj
        raw = dot(kv2[:, j * HD:(j + 1) * HD], qj, NT) * factor
        raw = jnp.where(allow, raw, NEG_BIG)
        dpo = dot(kv2[:, WIDTH + j * HD:WIDTH + (j + 1) * HD], gj, NT)
        top = jnp.max(raw, 0, keepdims=True)
        e = jnp.exp(raw - top)
        eown[j] = e
        dpown[j] = dpo
        stat[j, 0:1] = top
        stat[j, 1:2] = jnp.sum(e, 0, keepdims=True)
        stat[j, 2:3] = jnp.sum(e * dpo, 0, keepdims=True)
        gsum[j, 0:1] = jnp.sum(gj.astype(F32), 0, keepdims=True)

    for j in range(KVH):
        ready(j)

    def prompt(j):
        both = pre_all[j // STEP, :, :, (j % STEP) * 2 * HD:(j % STEP + 1) * 2 * HD].reshape(pre_rows, 2 * HD)
        return both[:, :HD], both[:, HD:]

    def keys_of(j):
        return jnp.concatenate([prompt(j)[0], kv2[:, j * HD:(j + 1) * HD]], axis=0)

    rows = []
    for j in range(KVH):
        if j % STEP == 0:
            take(pre_all.at[j // STEP, pl.ds(0, n_grp - 1)], ag_sem.at[1 + j // STEP])
        pk, pv = prompt(j)
        qj = q2[j]
        s_p = dot(pk, qj, NT) * factor
        dp_p = dot(pv, g2[j], NT)
        top_o = stat[j, 0:1]
        top = jnp.maximum(jnp.max(s_p, 0, keepdims=True), top_o)
        e_p = jnp.exp(s_p - top)
        shift = jnp.exp(top_o - top)
        inv = 1.0 / (jnp.sum(e_p, 0, keepdims=True) + shift * stat[j, 1:2])
        scale = shift * inv
        p_p = e_p * inv
        p_o = eown[j] * scale
        dp_o = dpown[j]
        row = jnp.sum(p_p * dp_p, 0, keepdims=True) + scale * stat[j, 2:3]
        ds = jnp.concatenate([(p_p * (dp_p - row)).astype(BF16), (p_o * (dp_o - row)).astype(BF16)], axis=0)
        pb = jnp.concatenate([p_p.astype(BF16), p_o.astype(BF16)], axis=0)
        pb_s[j] = pb
        ds_s[j] = ds
        heads = jnp.transpose(dot(ds, pick, NN))[:TILE]
        over = jnp.sum(ds.astype(F32), 0, keepdims=True)
        over_high = over.astype(BF16).astype(F32)
        over = jnp.concatenate([over_high, over - over_high, jnp.zeros((TILE - 2, GROUP * slots), F32)], axis=0).astype(BF16)
        key_sum = jnp.sum(dot(over, qj, NN), 0, keepdims=True) * factor
        high = heads.astype(BF16).astype(F32)
        split = dot(jnp.concatenate([high, heads - high], axis=0).astype(BF16), keys_of(j), NN) * factor
        block = split[:TILE] + split[TILE:]
        block = jnp.where(bias_row == GROUP, key_sum, block)
        rows.append(jnp.where(bias_row == GROUP + 1, gsum[j, 0:1], block))
        if j % STEP == STEP - 1:
            c = j // STEP
            b_all[c, slot] = jnp.concatenate(rows, axis=0).astype(BF16)
            rows = []
            for a, b in across:
                send(b_all.at[c, slot], b_all.at[c, slot], b_sem, 1 + c, at(a, b))
    for j in range(KVH):
        vc = slice(WIDTH + j * HD, WIDTH + (j + 1) * HD)
        kc = slice(j * HD, (j + 1) * HD)
        dkr = (dot(ds_s[j], q2[j], NN) * factor).astype(BF16)
        pg[:, :, kc] = dkr[:pre_rows].reshape(n_grp, own_rows, HD)
        dkv_s[:, kc] = dkr[pre_rows:]
        dvr = dot(pb_s[j], g2[j], NN).astype(BF16)
        pg[:, :, vc] = dvr[:pre_rows].reshape(n_grp, own_rows, HD)
        dkv_s[:, vc] = dvr[pre_rows:]
    for off in range(1, n_grp):
        peer = group(off)
        send(pg.at[peer["grp"]], pr.at[me], rs_sem, 1, peer)

    for j in range(KVH):
        dq = dot(ds_s[j], keys_of(j), TN) * factor
        vals = jnp.concatenate([prompt(j)[1], kv2[:, WIDTH + j * HD:WIDTH + (j + 1) * HD]], axis=0)
        out = dot(pb_s[j], vals, TN)
        for h in range(GROUP):
            here = slice((j * GROUP + h) * HD, (j * GROUP + h + 1) * HD)
            dq_s[:, here] = dq[h * slots:(h + 1) * slots].astype(BF16)
            att_s[:, here] = jnp.where(live_out, out[h * slots:(h + 1) * slots], 0.0).astype(BF16)

    take(pr.at[pl.ds(0, n_grp - 1)], rs_sem.at[1])
    pr[me] = pg[me]
    acc = pr[0].astype(F32)
    for k in range(1, n_grp):
        acc = acc + pr[k].astype(F32)
    dpre_ref[...] = acc.astype(BF16)

    for c in range(KVH // STEP):
        take(b_all.at[c, pl.ds(0, n_slots - 1)], b_sem.at[1 + c])
        total = b_all[c, 0].astype(F32)
        for k in range(1, n_slots):
            total = total + b_all[c, k].astype(F32)
        f_all[lane, c] = total
    for off in range(1, inner):
        send(f_all.at[lane], f_all.at[lane], f_sem, 1, part(off))
    take(pre_all.at[:, pl.ds(0, n_grp - 1)], ag_sem.at[0])
    take(pr.at[pl.ds(0, n_grp - 1)], rs_sem.at[0])
    take(b_all.at[:, pl.ds(0, n_slots - 1)], b_sem.at[0])
    take(f_all.at[pl.ds(0, inner - 1)], f_sem.at[0])
    take(f_all.at[pl.ds(0, inner - 1)], f_sem.at[1])
    for c in range(KVH // STEP):
        total = f_all[0, c]
        for k in range(1, inner):
            total = total + f_all[k, c]
        for k in range(STEP):
            j = c * STEP + k
            for h in range(GROUP):
                qsum_ref[pl.ds((j * GROUP + h) * HD, HD)] = total[k * TILE + h]
            kvsum_ref[pl.ds(j * HD, HD)] = total[k * TILE + GROUP]
            kvsum_ref[pl.ds(WIDTH + j * HD, HD)] = total[k * TILE + GROUP + 1]


def write_out(*refs):
    count = (len(refs) - 1) // 2
    copies = [pltpu.make_async_copy(refs[k], refs[count + k], refs[-1].at[k]) for k in range(count)]
    for item in copies:
        item.start()
    for item in copies:
        item.wait()


def local(n_grp, n_dp, query, resp_kv, prefix_kv, query_bias, kv_bias, out_grad, lengths):
    slots = query.shape[1]
    own_rows = prefix_kv.shape[1]
    pre_rows = own_rows * n_grp
    inner = 2 if n_grp % 2 == 0 and n_grp // 2 * n_dp <= DIRECT else n_grp
    n_slots = n_grp // inner * n_dp
    chunks = KVH // STEP
    qw = QH * HD
    kw = 2 * WIDTH
    hbm = pl.BlockSpec(memory_space=pltpu.HBM)
    vmem = pl.BlockSpec(memory_space=pltpu.VMEM)
    dma = lambda *n: pltpu.SemaphoreType.DMA(n)
    shapes = (
        jax.ShapeDtypeStruct((slots, qw), BF16),
        jax.ShapeDtypeStruct((slots, qw), BF16),
        jax.ShapeDtypeStruct((slots, kw), BF16),
        jax.ShapeDtypeStruct((own_rows, kw), BF16),
        jax.ShapeDtypeStruct((qw,), F32),
        jax.ShapeDtypeStruct((kw,), F32),
    )
    outs = pl.pallas_call(
        functools.partial(kernel, n_grp, n_dp, inner),
        name="replay",
        out_shape=shapes,
        in_specs=[pl.BlockSpec(memory_space=pltpu.SMEM)] + [hbm] * 6,
        out_specs=(vmem,) * 6,
        scratch_shapes=[
            pltpu.VMEM((own_rows, kw), BF16),
            pltpu.VMEM((qw,), F32),
            pltpu.VMEM((kw,), F32),
            pltpu.VMEM((slots, qw), BF16),
            pltpu.VMEM((slots, qw), BF16),
            pltpu.VMEM((slots, kw), BF16),
            pltpu.VMEM((KVH, GROUP * slots, HD), BF16),
            pltpu.VMEM((KVH, GROUP * slots, HD), BF16),
            pltpu.VMEM((slots, kw), BF16),
            pltpu.VMEM((KVH, slots, GROUP * slots), F32),
            pltpu.VMEM((KVH, slots, GROUP * slots), F32),
            pltpu.VMEM((KVH, TILE, GROUP * slots), F32),
            pltpu.VMEM((KVH, TILE, HD), F32),
            pltpu.VMEM((KVH, pre_rows + slots, GROUP * slots), BF16),
            pltpu.VMEM((KVH, pre_rows + slots, GROUP * slots), BF16),
            pltpu.VMEM((chunks, n_grp, own_rows, STEP * 2 * HD), BF16),
            pltpu.VMEM((n_grp, own_rows, kw), BF16),
            pltpu.VMEM((n_grp, own_rows, kw), BF16),
            pltpu.VMEM((chunks, n_slots, STEP * TILE, HD), BF16),
            pltpu.VMEM((inner, chunks, STEP * TILE, HD), F32),
            dma(6), dma(1 + chunks), dma(2), dma(1 + chunks), dma(2),
        ],
        compiler_params=pltpu.CompilerParams(
            collective_id=0, has_side_effects=True, vmem_limit_bytes=24 * 1024 * 1024
        ),
    )(lengths, *(pltpu.with_memory_space_constraint(x, pltpu.HBM) for x in (query[0], resp_kv[0], prefix_kv[0], query_bias, kv_bias, out_grad[0])))
    att, dq, dkv, dpre, qsum, kvsum = pl.pallas_call(
        write_out,
        name="write_out",
        out_shape=shapes,
        in_specs=[vmem] * 6,
        out_specs=(hbm,) * 6,
        scratch_shapes=[dma(6)],
        compiler_params=pltpu.CompilerParams(vmem_limit_bytes=1024 * 1024),
    )(*outs)
    return att[None], dq[None], dkv[None], dpre[None], qsum, kvsum


def solution(mesh):
    return jax.shard_map(
        functools.partial(local, mesh.shape["grp"], mesh.shape["dp"]),
        mesh=mesh,
        in_specs=(
            P("dp", "grp", None),
            P("dp", "grp", None),
            P("dp", "grp", None),
            P(),
            P(),
            P("dp", "grp", None),
            P("dp", "grp"),
        ),
        out_specs=(
            P("dp", "grp", None),
            P("dp", "grp", None),
            P("dp", "grp", None),
            P("dp", "grp", None),
            P(),
            P(),
        ),
        check_vma=False,
    )
```

```python
import functools

import jax
import jax.numpy as jnp
from jax import lax
from jax.experimental import pallas as pl
from jax.experimental.pallas import tpu as pltpu
from jax.sharding import PartitionSpec as P

QH = 20
KVH = 4
STEP = 2
HD = 128
NEG_BIG = -1e30
TILE = 8
DIRECT = 32
GROUP = QH // KVH
WIDTH = KVH * HD
GCOLS = GROUP * HD
MESH = pl.DeviceIdType.MESH
F32 = jnp.float32
BF16 = jnp.bfloat16

NT = (((1,), (1,)), ((), ()))
NN = (((1,), (0,)), ((), ()))
TN = (((0,), (0,)), ((), ()))


def dot(a, b, dims):
    return lax.dot_general(a, b, dims, preferred_element_type=F32)


def heads_down(x):
    return jnp.concatenate([x[:, h * HD:(h + 1) * HD] for h in range(GROUP)], axis=0)


def kernel(
    n_grp, n_dp, inner,
    len_ref, q_hbm, kv_hbm, pre_hbm, qb_hbm, kvb_hbm, g_hbm,
    att_s, dq_s, dkv_s, dpre_ref, qsum_ref, kvsum_ref,
    pre_ref, qb_ref, kvb_ref, q_s, g_s, kv_s, q2, g2, kv2, eown, dpown, stat, gsum, pb_s, ds_s,
    pre_all, pg, pr, b_all, f_all,
    in_sem, ag_sem, rs_sem, b_sem, f_sem,
):
    me = lax.axis_index("grp")
    my = lax.axis_index("dp")
    factor = HD ** (-0.5)
    slots = q_s.shape[0]
    own_rows = pre_ref.shape[0]
    pre_rows = n_grp * own_rows
    outer = n_grp // inner
    lane = lax.rem(me, inner)
    row_of = lax.div(me, inner)
    slot = row_of * n_dp + my
    n_slots = outer * n_dp

    across = [(a, b) for b in range(1, n_dp) for a in range(outer)] + [(a, 0) for a in range(1, outer)]

    def at(a, b):
        return {"grp": lax.rem(row_of + a, outer) * inner + lane, "dp": lax.rem(my + b, n_dp)}

    def group(off):
        return {"grp": lax.rem(me + off, n_grp), "dp": my}

    def part(off):
        return {"grp": row_of * inner + lax.rem(lane + off, inner), "dp": my}

    loads = [
        pltpu.make_async_copy(src, dst, in_sem.at[k])
        for k, (src, dst) in enumerate((
            (pre_hbm, pre_ref), (kvb_hbm, kvb_ref), (qb_hbm, qb_ref), (kv_hbm, kv_s), (q_hbm, q_s), (g_hbm, g_s)))
    ]
    for item in loads[:2]:
        item.start()
    barrier = pltpu.get_barrier_semaphore()
    for off in range(1, n_grp):
        pl.semaphore_signal(barrier, inc=1, device_id=group(off), device_id_type=MESH)
    far = [at(a, b) for a, b in across if b > 0]
    for peer in far:
        pl.semaphore_signal(barrier, inc=1, device_id=peer, device_id_type=MESH)
    for item in loads[2:]:
        item.start()

    loads[0].wait()
    loads[1].wait()
    kvb = kvb_ref[...].reshape(1, 2 * WIDTH)
    mine = (pre_ref[...].astype(F32) + kvb).astype(BF16)
    for j in range(KVH):
        pre_all[j // STEP, me, :, (j % STEP) * 2 * HD:(j % STEP + 1) * 2 * HD] = jnp.concatenate(
            [mine[:, j * HD:(j + 1) * HD], mine[:, WIDTH + j * HD:WIDTH + (j + 1) * HD]], axis=1)

    def send(src, dst, sems, recv, peer):
        pltpu.make_async_remote_copy(
            src_ref=src, dst_ref=dst, send_sem=sems.at[0], recv_sem=sems.at[recv],
            device_id=peer, device_id_type=MESH).start()

    def take(like, sem):
        pltpu.make_async_copy(like, like, sem).wait()

    pl.semaphore_wait(barrier, n_grp - 1 + len(far))
    for c in range(KVH // STEP):
        for off in range(1, n_grp):
            send(pre_all.at[c, me], pre_all.at[c, me], ag_sem, 1 + c, group(off))

    length = len_ref[0, 0]
    live_in = lax.broadcasted_iota(jnp.int32, (slots, GCOLS), 0) < length
    live_out = lax.broadcasted_iota(jnp.int32, (slots, HD), 0) < length
    key_at = lax.broadcasted_iota(jnp.int32, (slots, slots), 0)
    row_at = lax.broadcasted_iota(jnp.int32, (slots, slots), 1)
    allow = jnp.concatenate([key_at <= row_at] * GROUP, axis=1)
    pick = (lax.broadcasted_iota(jnp.int32, (GROUP * slots, HD), 1)
            == lax.div(lax.broadcasted_iota(jnp.int32, (GROUP * slots, HD), 0), slots)).astype(F32).astype(BF16)
    bias_row = lax.broadcasted_iota(jnp.int32, (TILE, HD), 0)

    for item in loads[2:]:
        item.wait()
    kv2[...] = (kv_s[...].astype(F32) + kvb).astype(BF16)
    qb = qb_ref[...].reshape(1, QH * HD)
    def ready(j):
        cols = slice(j * GCOLS, (j + 1) * GCOLS)
        qj = heads_down((q_s[:, cols].astype(F32) + qb[:, cols]).astype(BF16))
        gj = g_s[:, cols]
        gj = heads_down(jnp.where(live_in, gj, jnp.zeros_like(gj)))
        q2[j] = qj
        g2[j] = gj
        raw = dot(kv2[:, j * HD:(j + 1) * HD], qj, NT) * factor
        raw = jnp.where(allow, raw, NEG_BIG)
        dpo = dot(kv2[:, WIDTH + j * HD:WIDTH + (j + 1) * HD], gj, NT)
        top = jnp.max(raw, 0, keepdims=True)
        e = jnp.exp(raw - top)
        eown[j] = e
        dpown[j] = dpo
        stat[j, 0:1] = top
        stat[j, 1:2] = jnp.sum(e, 0, keepdims=True)
        stat[j, 2:3] = jnp.sum(e * dpo, 0, keepdims=True)
        gsum[j, 0:1] = jnp.sum(gj.astype(F32), 0, keepdims=True)

    for j in range(KVH):
        ready(j)

    def prompt(j):
        both = pre_all[j // STEP, :, :, (j % STEP) * 2 * HD:(j % STEP + 1) * 2 * HD].reshape(pre_rows, 2 * HD)
        return both[:, :HD], both[:, HD:]

    def keys_of(j):
        return jnp.concatenate([prompt(j)[0], kv2[:, j * HD:(j + 1) * HD]], axis=0)

    rows = []
    for j in range(KVH):
        if j % STEP == 0:
            take(pre_all.at[j // STEP, pl.ds(0, n_grp - 1)], ag_sem.at[1 + j // STEP])
        pk, pv = prompt(j)
        qj = q2[j]
        s_p = dot(pk, qj, NT) * factor
        dp_p = dot(pv, g2[j], NT)
        top_o = stat[j, 0:1]
        top = jnp.maximum(jnp.max(s_p, 0, keepdims=True), top_o)
        e_p = jnp.exp(s_p - top)
        shift = jnp.exp(top_o - top)
        inv = 1.0 / (jnp.sum(e_p, 0, keepdims=True) + shift * stat[j, 1:2])
        scale = shift * inv
        p_p = e_p * inv
        p_o = eown[j] * scale
        dp_o = dpown[j]
        row = jnp.sum(p_p * dp_p, 0, keepdims=True) + scale * stat[j, 2:3]
        ds = jnp.concatenate([(p_p * (dp_p - row)).astype(BF16), (p_o * (dp_o - row)).astype(BF16)], axis=0)
        pb = jnp.concatenate([p_p.astype(BF16), p_o.astype(BF16)], axis=0)
        pb_s[j] = pb
        ds_s[j] = ds
        heads = jnp.transpose(dot(ds, pick, NN))[:TILE]
        over = jnp.sum(ds.astype(F32), 0, keepdims=True)
        over_high = over.astype(BF16).astype(F32)
        over = jnp.concatenate([over_high, over - over_high, jnp.zeros((TILE - 2, GROUP * slots), F32)], axis=0).astype(BF16)
        key_sum = jnp.sum(dot(over, qj, NN), 0, keepdims=True) * factor
        high = heads.astype(BF16).astype(F32)
        split = dot(jnp.concatenate([high, heads - high], axis=0).astype(BF16), keys_of(j), NN) * factor
        block = split[:TILE] + split[TILE:]
        block = jnp.where(bias_row == GROUP, key_sum, block)
        rows.append(jnp.where(bias_row == GROUP + 1, gsum[j, 0:1], block))
        if j % STEP == STEP - 1:
            c = j // STEP
            b_all[c, slot] = jnp.concatenate(rows, axis=0).astype(BF16)
            rows = []
            for a, b in across:
                send(b_all.at[c, slot], b_all.at[c, slot], b_sem, 1 + c, at(a, b))
    for j in range(KVH):
        vc = slice(WIDTH + j * HD, WIDTH + (j + 1) * HD)
        kc = slice(j * HD, (j + 1) * HD)
        dkr = (dot(ds_s[j], q2[j], NN) * factor).astype(BF16)
        pg[:, :, kc] = dkr[:pre_rows].reshape(n_grp, own_rows, HD)
        dkv_s[:, kc] = dkr[pre_rows:]
        dvr = dot(pb_s[j], g2[j], NN).astype(BF16)
        pg[:, :, vc] = dvr[:pre_rows].reshape(n_grp, own_rows, HD)
        dkv_s[:, vc] = dvr[pre_rows:]
    for off in range(1, n_grp):
        peer = group(off)
        send(pg.at[peer["grp"]], pr.at[me], rs_sem, 1, peer)

    for j in range(KVH):
        dq = dot(ds_s[j], keys_of(j), TN) * factor
        vals = jnp.concatenate([prompt(j)[1], kv2[:, WIDTH + j * HD:WIDTH + (j + 1) * HD]], axis=0)
        out = dot(pb_s[j], vals, TN)
        for h in range(GROUP):
            here = slice((j * GROUP + h) * HD, (j * GROUP + h + 1) * HD)
            dq_s[:, here] = dq[h * slots:(h + 1) * slots].astype(BF16)
            att_s[:, here] = jnp.where(live_out, out[h * slots:(h + 1) * slots], 0.0).astype(BF16)

    for c in range(KVH // STEP):
        take(b_all.at[c, pl.ds(0, n_slots - 1)], b_sem.at[1 + c])
        total = b_all[c, 0].astype(F32)
        for k in range(1, n_slots):
            total = total + b_all[c, k].astype(F32)
        f_all[lane, c] = total
    for off in range(1, inner):
        send(f_all.at[lane], f_all.at[lane], f_sem, 1, part(off))
    take(pr.at[pl.ds(0, n_grp - 1)], rs_sem.at[1])
    pr[me] = pg[me]
    acc = pr[0].astype(F32)
    for k in range(1, n_grp):
        acc = acc + pr[k].astype(F32)
    dpre_ref[...] = acc.astype(BF16)
    take(pre_all.at[:, pl.ds(0, n_grp - 1)], ag_sem.at[0])
    take(pr.at[pl.ds(0, n_grp - 1)], rs_sem.at[0])
    take(b_all.at[:, pl.ds(0, n_slots - 1)], b_sem.at[0])
    take(f_all.at[pl.ds(0, inner - 1)], f_sem.at[0])
    take(f_all.at[pl.ds(0, inner - 1)], f_sem.at[1])
    for c in range(KVH // STEP):
        total = f_all[0, c]
        for k in range(1, inner):
            total = total + f_all[k, c]
        for k in range(STEP):
            j = c * STEP + k
            for h in range(GROUP):
                qsum_ref[pl.ds((j * GROUP + h) * HD, HD)] = total[k * TILE + h]
            kvsum_ref[pl.ds(j * HD, HD)] = total[k * TILE + GROUP]
            kvsum_ref[pl.ds(WIDTH + j * HD, HD)] = total[k * TILE + GROUP + 1]


def write_out(*refs):
    count = (len(refs) - 1) // 2
    copies = [pltpu.make_async_copy(refs[k], refs[count + k], refs[-1].at[k]) for k in range(count)]
    for item in copies:
        item.start()
    for item in copies:
        item.wait()


def local(n_grp, n_dp, query, resp_kv, prefix_kv, query_bias, kv_bias, out_grad, lengths):
    slots = query.shape[1]
    own_rows = prefix_kv.shape[1]
    pre_rows = own_rows * n_grp
    inner = 2 if n_grp % 2 == 0 and n_grp // 2 * n_dp <= DIRECT else n_grp
    n_slots = n_grp // inner * n_dp
    chunks = KVH // STEP
    qw = QH * HD
    kw = 2 * WIDTH
    hbm = pl.BlockSpec(memory_space=pltpu.HBM)
    vmem = pl.BlockSpec(memory_space=pltpu.VMEM)
    dma = lambda *n: pltpu.SemaphoreType.DMA(n)
    shapes = (
        jax.ShapeDtypeStruct((slots, qw), BF16),
        jax.ShapeDtypeStruct((slots, qw), BF16),
        jax.ShapeDtypeStruct((slots, kw), BF16),
        jax.ShapeDtypeStruct((own_rows, kw), BF16),
        jax.ShapeDtypeStruct((qw,), F32),
        jax.ShapeDtypeStruct((kw,), F32),
    )
    outs = pl.pallas_call(
        functools.partial(kernel, n_grp, n_dp, inner),
        name="replay",
        out_shape=shapes,
        in_specs=[pl.BlockSpec(memory_space=pltpu.SMEM)] + [hbm] * 6,
        out_specs=(vmem,) * 6,
        scratch_shapes=[
            pltpu.VMEM((own_rows, kw), BF16),
            pltpu.VMEM((qw,), F32),
            pltpu.VMEM((kw,), F32),
            pltpu.VMEM((slots, qw), BF16),
            pltpu.VMEM((slots, qw), BF16),
            pltpu.VMEM((slots, kw), BF16),
            pltpu.VMEM((KVH, GROUP * slots, HD), BF16),
            pltpu.VMEM((KVH, GROUP * slots, HD), BF16),
            pltpu.VMEM((slots, kw), BF16),
            pltpu.VMEM((KVH, slots, GROUP * slots), F32),
            pltpu.VMEM((KVH, slots, GROUP * slots), F32),
            pltpu.VMEM((KVH, TILE, GROUP * slots), F32),
            pltpu.VMEM((KVH, TILE, HD), F32),
            pltpu.VMEM((KVH, pre_rows + slots, GROUP * slots), BF16),
            pltpu.VMEM((KVH, pre_rows + slots, GROUP * slots), BF16),
            pltpu.VMEM((chunks, n_grp, own_rows, STEP * 2 * HD), BF16),
            pltpu.VMEM((n_grp, own_rows, kw), BF16),
            pltpu.VMEM((n_grp, own_rows, kw), BF16),
            pltpu.VMEM((chunks, n_slots, STEP * TILE, HD), BF16),
            pltpu.VMEM((inner, chunks, STEP * TILE, HD), F32),
            dma(6), dma(1 + chunks), dma(2), dma(1 + chunks), dma(2),
        ],
        compiler_params=pltpu.CompilerParams(
            collective_id=0, has_side_effects=True, vmem_limit_bytes=24 * 1024 * 1024
        ),
    )(lengths, *(pltpu.with_memory_space_constraint(x, pltpu.HBM) for x in (query[0], resp_kv[0], prefix_kv[0], query_bias, kv_bias, out_grad[0])))
    att, dq, dkv, dpre, qsum, kvsum = pl.pallas_call(
        write_out,
        name="write_out",
        out_shape=shapes,
        in_specs=[vmem] * 6,
        out_specs=(hbm,) * 6,
        scratch_shapes=[dma(6)],
        compiler_params=pltpu.CompilerParams(vmem_limit_bytes=1024 * 1024),
    )(*outs)
    return att[None], dq[None], dkv[None], dpre[None], qsum, kvsum


def solution(mesh):
    return jax.shard_map(
        functools.partial(local, mesh.shape["grp"], mesh.shape["dp"]),
        mesh=mesh,
        in_specs=(
            P("dp", "grp", None),
            P("dp", "grp", None),
            P("dp", "grp", None),
            P(),
            P(),
            P("dp", "grp", None),
            P("dp", "grp"),
        ),
        out_specs=(
            P("dp", "grp", None),
            P("dp", "grp", None),
            P("dp", "grp", None),
            P("dp", "grp", None),
            P(),
            P(),
        ),
        check_vma=False,
    )
```

```python
import functools

import jax
import jax.numpy as jnp
from jax import lax
from jax.experimental import pallas as pl
from jax.experimental.pallas import tpu as pltpu
from jax.sharding import PartitionSpec as P

QH = 20
KVH = 4
STEP = 2
HD = 128
NEG_BIG = -1e30
TILE = 8
DIRECT = 32
GROUP = QH // KVH
WIDTH = KVH * HD
GCOLS = GROUP * HD
MESH = pl.DeviceIdType.MESH
F32 = jnp.float32
BF16 = jnp.bfloat16

NT = (((1,), (1,)), ((), ()))
NN = (((1,), (0,)), ((), ()))
TN = (((0,), (0,)), ((), ()))


def dot(a, b, dims):
    return lax.dot_general(a, b, dims, preferred_element_type=F32)


def heads_down(x):
    return jnp.concatenate([x[:, h * HD:(h + 1) * HD] for h in range(GROUP)], axis=0)


def kernel(
    n_grp, n_dp, inner,
    len_ref, q_hbm, kv_hbm, pre_hbm, qb_hbm, kvb_hbm, g_hbm,
    att_s, dq_s, dkv_s, dpre_ref, qsum_ref, kvsum_ref,
    pre_ref, qb_ref, kvb_ref, q_s, g_s, kv_s, q2, g2, kv2, eown, dpown, stat, gsum, pb_s, ds_s,
    pre_all, pg, pr, b_all, f_all,
    in_sem, ag_sem, rs_sem, b_sem, f_sem,
):
    me = lax.axis_index("grp")
    my = lax.axis_index("dp")
    factor = HD ** (-0.5)
    slots = q_s.shape[0]
    own_rows = pre_ref.shape[0]
    pre_rows = n_grp * own_rows
    outer = n_grp // inner
    lane = lax.rem(me, inner)
    row_of = lax.div(me, inner)
    slot = row_of * n_dp + my
    n_slots = outer * n_dp

    across = [(a, b) for b in range(1, n_dp) for a in reversed(range(outer))] + [(a, 0) for a in range(1, outer)]

    def at(a, b):
        return {"grp": lax.rem(row_of + a, outer) * inner + lane, "dp": lax.rem(my + b, n_dp)}

    def group(off):
        return {"grp": lax.rem(me + off, n_grp), "dp": my}

    def part(off):
        return {"grp": row_of * inner + lax.rem(lane + off, inner), "dp": my}

    loads = [
        pltpu.make_async_copy(src, dst, in_sem.at[k])
        for k, (src, dst) in enumerate((
            (pre_hbm, pre_ref), (kvb_hbm, kvb_ref), (qb_hbm, qb_ref), (kv_hbm, kv_s), (q_hbm, q_s), (g_hbm, g_s)))
    ]
    for item in loads[:2]:
        item.start()
    barrier = pltpu.get_barrier_semaphore()
    for off in range(1, n_grp):
        pl.semaphore_signal(barrier, inc=1, device_id=group(off), device_id_type=MESH)
    far = [at(a, b) for a, b in across if b > 0]
    for peer in far:
        pl.semaphore_signal(barrier, inc=1, device_id=peer, device_id_type=MESH)
    for item in loads[2:]:
        item.start()

    loads[0].wait()
    loads[1].wait()
    kvb = kvb_ref[...].reshape(1, 2 * WIDTH)
    mine = (pre_ref[...].astype(F32) + kvb).astype(BF16)
    for j in range(KVH):
        pre_all[j // STEP, me, :, (j % STEP) * 2 * HD:(j % STEP + 1) * 2 * HD] = jnp.concatenate(
            [mine[:, j * HD:(j + 1) * HD], mine[:, WIDTH + j * HD:WIDTH + (j + 1) * HD]], axis=1)

    def send(src, dst, sems, recv, peer):
        pltpu.make_async_remote_copy(
            src_ref=src, dst_ref=dst, send_sem=sems.at[0], recv_sem=sems.at[recv],
            device_id=peer, device_id_type=MESH).start()

    def take(like, sem):
        pltpu.make_async_copy(like, like, sem).wait()

    pl.semaphore_wait(barrier, n_grp - 1 + len(far))
    for c in range(KVH // STEP):
        for off in range(1, n_grp):
            send(pre_all.at[c, me], pre_all.at[c, me], ag_sem, 1 + c, group(off))

    length = len_ref[0, 0]
    live_in = lax.broadcasted_iota(jnp.int32, (slots, GCOLS), 0) < length
    live_out = lax.broadcasted_iota(jnp.int32, (slots, HD), 0) < length
    key_at = lax.broadcasted_iota(jnp.int32, (slots, slots), 0)
    row_at = lax.broadcasted_iota(jnp.int32, (slots, slots), 1)
    allow = jnp.concatenate([key_at <= row_at] * GROUP, axis=1)
    pick = (lax.broadcasted_iota(jnp.int32, (GROUP * slots, HD), 1)
            == lax.div(lax.broadcasted_iota(jnp.int32, (GROUP * slots, HD), 0), slots)).astype(F32).astype(BF16)
    bias_row = lax.broadcasted_iota(jnp.int32, (TILE, HD), 0)

    for item in loads[2:]:
        item.wait()
    kv2[...] = (kv_s[...].astype(F32) + kvb).astype(BF16)
    qb = qb_ref[...].reshape(1, QH * HD)
    def ready(j):
        cols = slice(j * GCOLS, (j + 1) * GCOLS)
        qj = heads_down((q_s[:, cols].astype(F32) + qb[:, cols]).astype(BF16))
        gj = g_s[:, cols]
        gj = heads_down(jnp.where(live_in, gj, jnp.zeros_like(gj)))
        q2[j] = qj
        g2[j] = gj
        raw = dot(kv2[:, j * HD:(j + 1) * HD], qj, NT) * factor
        raw = jnp.where(allow, raw, NEG_BIG)
        dpo = dot(kv2[:, WIDTH + j * HD:WIDTH + (j + 1) * HD], gj, NT)
        top = jnp.max(raw, 0, keepdims=True)
        e = jnp.exp(raw - top)
        eown[j] = e
        dpown[j] = dpo
        stat[j, 0:1] = top
        stat[j, 1:2] = jnp.sum(e, 0, keepdims=True)
        stat[j, 2:3] = jnp.sum(e * dpo, 0, keepdims=True)
        gsum[j, 0:1] = jnp.sum(gj.astype(F32), 0, keepdims=True)

    for j in range(KVH):
        ready(j)

    def prompt(j):
        both = pre_all[j // STEP, :, :, (j % STEP) * 2 * HD:(j % STEP + 1) * 2 * HD].reshape(pre_rows, 2 * HD)
        return both[:, :HD], both[:, HD:]

    def keys_of(j):
        return jnp.concatenate([prompt(j)[0], kv2[:, j * HD:(j + 1) * HD]], axis=0)

    rows = []
    for j in range(KVH):
        if j % STEP == 0:
            take(pre_all.at[j // STEP, pl.ds(0, n_grp - 1)], ag_sem.at[1 + j // STEP])
        pk, pv = prompt(j)
        qj = q2[j]
        s_p = dot(pk, qj, NT) * factor
        dp_p = dot(pv, g2[j], NT)
        top_o = stat[j, 0:1]
        top = jnp.maximum(jnp.max(s_p, 0, keepdims=True), top_o)
        e_p = jnp.exp(s_p - top)
        shift = jnp.exp(top_o - top)
        inv = 1.0 / (jnp.sum(e_p, 0, keepdims=True) + shift * stat[j, 1:2])
        scale = shift * inv
        p_p = e_p * inv
        p_o = eown[j] * scale
        dp_o = dpown[j]
        row = jnp.sum(p_p * dp_p, 0, keepdims=True) + scale * stat[j, 2:3]
        ds = jnp.concatenate([(p_p * (dp_p - row)).astype(BF16), (p_o * (dp_o - row)).astype(BF16)], axis=0)
        pb_s[j, :pre_rows] = p_p.astype(BF16)
        stat[j, 3:4] = scale
        ds_s[j] = ds
        heads = dot(ds, pick, NN)
        keys_f = keys_of(j).astype(F32)
        over = jnp.sum(ds.astype(F32), 0, keepdims=True)
        over_high = over.astype(BF16).astype(F32)
        over = jnp.concatenate([over_high, over - over_high, jnp.zeros((TILE - 2, GROUP * slots), F32)], axis=0).astype(BF16)
        key_sum = jnp.sum(dot(over, qj, NN), 0, keepdims=True) * factor
        block = jnp.zeros((TILE, HD), F32)
        for h in range(GROUP):
            part_sum = jnp.sum(heads[:, h:h + 1] * keys_f, 0, keepdims=True) * factor
            block = jnp.where(bias_row == h, part_sum, block)
        block = jnp.where(bias_row == GROUP, key_sum, block)
        rows.append(jnp.where(bias_row == GROUP + 1, gsum[j, 0:1], block))
        if j % STEP == STEP - 1:
            c = j // STEP
            b_all[c, slot] = jnp.concatenate(rows, axis=0).astype(BF16)
            rows = []
            for a, b in across:
                send(b_all.at[c, slot], b_all.at[c, slot], b_sem, 1 + c, at(a, b))
    for j in range(KVH):
        vc = slice(WIDTH + j * HD, WIDTH + (j + 1) * HD)
        kc = slice(j * HD, (j + 1) * HD)
        dkr = (dot(ds_s[j], q2[j], NN) * factor).astype(BF16)
        pg[:, :, kc] = dkr[:pre_rows].reshape(n_grp, own_rows, HD)
        dkv_s[:, kc] = dkr[pre_rows:]
        pb_s[j, pre_rows:] = (eown[j] * stat[j, 3:4]).astype(BF16)
        dvr = dot(pb_s[j], g2[j], NN).astype(BF16)
        pg[:, :, vc] = dvr[:pre_rows].reshape(n_grp, own_rows, HD)
        dkv_s[:, vc] = dvr[pre_rows:]
    for off in range(1, n_grp):
        peer = group(off)
        send(pg.at[peer["grp"]], pr.at[me], rs_sem, 1, peer)

    for j in range(KVH):
        dq = dot(ds_s[j], keys_of(j), TN) * factor
        vals = jnp.concatenate([prompt(j)[1], kv2[:, WIDTH + j * HD:WIDTH + (j + 1) * HD]], axis=0)
        out = dot(pb_s[j], vals, TN)
        for h in range(GROUP):
            here = slice((j * GROUP + h) * HD, (j * GROUP + h + 1) * HD)
            dq_s[:, here] = dq[h * slots:(h + 1) * slots].astype(BF16)
            att_s[:, here] = jnp.where(live_out, out[h * slots:(h + 1) * slots], 0.0).astype(BF16)

    for c in range(KVH // STEP):
        take(b_all.at[c, pl.ds(0, n_slots - 1)], b_sem.at[1 + c])
        total = b_all[c, 0].astype(F32)
        for k in range(1, n_slots):
            total = total + b_all[c, k].astype(F32)
        f_all[lane, c] = total
    for off in range(1, inner):
        send(f_all.at[lane], f_all.at[lane], f_sem, 1, part(off))
    take(pr.at[pl.ds(0, n_grp - 1)], rs_sem.at[1])
    pr[me] = pg[me]
    acc = pr[0].astype(F32)
    for k in range(1, n_grp):
        acc = acc + pr[k].astype(F32)
    dpre_ref[...] = acc.astype(BF16)
    take(pre_all.at[:, pl.ds(0, n_grp - 1)], ag_sem.at[0])
    take(pr.at[pl.ds(0, n_grp - 1)], rs_sem.at[0])
    take(b_all.at[:, pl.ds(0, n_slots - 1)], b_sem.at[0])
    take(f_all.at[pl.ds(0, inner - 1)], f_sem.at[0])
    take(f_all.at[pl.ds(0, inner - 1)], f_sem.at[1])
    for c in range(KVH // STEP):
        total = f_all[0, c]
        for k in range(1, inner):
            total = total + f_all[k, c]
        for k in range(STEP):
            j = c * STEP + k
            for h in range(GROUP):
                qsum_ref[pl.ds((j * GROUP + h) * HD, HD)] = total[k * TILE + h]
            kvsum_ref[pl.ds(j * HD, HD)] = total[k * TILE + GROUP]
            kvsum_ref[pl.ds(WIDTH + j * HD, HD)] = total[k * TILE + GROUP + 1]


def write_out(*refs):
    count = (len(refs) - 1) // 2
    copies = [pltpu.make_async_copy(refs[k], refs[count + k], refs[-1].at[k]) for k in range(count)]
    for item in copies:
        item.start()
    for item in copies:
        item.wait()


def local(n_grp, n_dp, query, resp_kv, prefix_kv, query_bias, kv_bias, out_grad, lengths):
    slots = query.shape[1]
    own_rows = prefix_kv.shape[1]
    pre_rows = own_rows * n_grp
    inner = 2 if n_grp % 2 == 0 and n_grp // 2 * n_dp <= DIRECT else n_grp
    n_slots = n_grp // inner * n_dp
    chunks = KVH // STEP
    qw = QH * HD
    kw = 2 * WIDTH
    hbm = pl.BlockSpec(memory_space=pltpu.HBM)
    vmem = pl.BlockSpec(memory_space=pltpu.VMEM)
    dma = lambda *n: pltpu.SemaphoreType.DMA(n)
    shapes = (
        jax.ShapeDtypeStruct((slots, qw), BF16),
        jax.ShapeDtypeStruct((slots, qw), BF16),
        jax.ShapeDtypeStruct((slots, kw), BF16),
        jax.ShapeDtypeStruct((own_rows, kw), BF16),
        jax.ShapeDtypeStruct((qw,), F32),
        jax.ShapeDtypeStruct((kw,), F32),
    )
    outs = pl.pallas_call(
        functools.partial(kernel, n_grp, n_dp, inner),
        name="replay",
        out_shape=shapes,
        in_specs=[pl.BlockSpec(memory_space=pltpu.SMEM)] + [hbm] * 6,
        out_specs=(vmem,) * 6,
        scratch_shapes=[
            pltpu.VMEM((own_rows, kw), BF16),
            pltpu.VMEM((qw,), F32),
            pltpu.VMEM((kw,), F32),
            pltpu.VMEM((slots, qw), BF16),
            pltpu.VMEM((slots, qw), BF16),
            pltpu.VMEM((slots, kw), BF16),
            pltpu.VMEM((KVH, GROUP * slots, HD), BF16),
            pltpu.VMEM((KVH, GROUP * slots, HD), BF16),
            pltpu.VMEM((slots, kw), BF16),
            pltpu.VMEM((KVH, slots, GROUP * slots), F32),
            pltpu.VMEM((KVH, slots, GROUP * slots), F32),
            pltpu.VMEM((KVH, TILE, GROUP * slots), F32),
            pltpu.VMEM((KVH, TILE, HD), F32),
            pltpu.VMEM((KVH, pre_rows + slots, GROUP * slots), BF16),
            pltpu.VMEM((KVH, pre_rows + slots, GROUP * slots), BF16),
            pltpu.VMEM((chunks, n_grp, own_rows, STEP * 2 * HD), BF16),
            pltpu.VMEM((n_grp, own_rows, kw), BF16),
            pltpu.VMEM((n_grp, own_rows, kw), BF16),
            pltpu.VMEM((chunks, n_slots, STEP * TILE, HD), BF16),
            pltpu.VMEM((inner, chunks, STEP * TILE, HD), F32),
            dma(6), dma(1 + chunks), dma(2), dma(1 + chunks), dma(2),
        ],
        compiler_params=pltpu.CompilerParams(
            collective_id=0, has_side_effects=True, vmem_limit_bytes=24 * 1024 * 1024
        ),
    )(lengths, *(pltpu.with_memory_space_constraint(x, pltpu.HBM) for x in (query[0], resp_kv[0], prefix_kv[0], query_bias, kv_bias, out_grad[0])))
    att, dq, dkv, dpre, qsum, kvsum = pl.pallas_call(
        write_out,
        name="write_out",
        out_shape=shapes,
        in_specs=[vmem] * 6,
        out_specs=(hbm,) * 6,
        scratch_shapes=[dma(6)],
        compiler_params=pltpu.CompilerParams(vmem_limit_bytes=1024 * 1024),
    )(*outs)
    return att[None], dq[None], dkv[None], dpre[None], qsum, kvsum


def solution(mesh):
    return jax.shard_map(
        functools.partial(local, mesh.shape["grp"], mesh.shape["dp"]),
        mesh=mesh,
        in_specs=(
            P("dp", "grp", None),
            P("dp", "grp", None),
            P("dp", "grp", None),
            P(),
            P(),
            P("dp", "grp", None),
            P("dp", "grp"),
        ),
        out_specs=(
            P("dp", "grp", None),
            P("dp", "grp", None),
            P("dp", "grp", None),
            P("dp", "grp", None),
            P(),
            P(),
        ),
        check_vma=False,
    )
```

```python
import functools

import jax
import jax.numpy as jnp
from jax import lax
from jax.experimental import pallas as pl
from jax.experimental.pallas import tpu as pltpu
from jax.sharding import PartitionSpec as P

QH = 20
KVH = 4
STEP = 2
HD = 128
NEG_BIG = -1e30
TILE = 8
DIRECT = 32
GROUP = QH // KVH
WIDTH = KVH * HD
GCOLS = GROUP * HD
MESH = pl.DeviceIdType.MESH
F32 = jnp.float32
BF16 = jnp.bfloat16

NT = (((1,), (1,)), ((), ()))
NN = (((1,), (0,)), ((), ()))
TN = (((0,), (0,)), ((), ()))


def dot(a, b, dims):
    return lax.dot_general(a, b, dims, preferred_element_type=F32)


def heads_down(x):
    return jnp.concatenate([x[:, h * HD:(h + 1) * HD] for h in range(GROUP)], axis=0)


def kernel(
    n_grp, n_dp, inner,
    len_ref, q_hbm, kv_hbm, pre_hbm, qb_hbm, kvb_hbm, g_hbm,
    att_s, dq_s, dkv_s, dpre_ref, qsum_ref, kvsum_ref,
    pre_ref, qb_ref, kvb_ref, q_s, g_s, kv_s, q2, g2, kv2, eown, dpown, stat, gsum, pb_s, ds_s,
    pre_all, pg, pr, b_all, f_all,
    in_sem, ag_sem, rs_sem, b_sem, f_sem,
):
    me = lax.axis_index("grp")
    my = lax.axis_index("dp")
    factor = HD ** (-0.5)
    slots = q_s.shape[0]
    own_rows = pre_ref.shape[0]
    pre_rows = n_grp * own_rows
    outer = n_grp // inner
    lane = lax.rem(me, inner)
    row_of = lax.div(me, inner)
    slot = row_of * n_dp + my
    n_slots = outer * n_dp

    across = [(a, b) for b in range(1, n_dp) for a in reversed(range(outer))] + [(a, 0) for a in range(1, outer)]

    def at(a, b):
        return {"grp": lax.rem(row_of + a, outer) * inner + lane, "dp": lax.rem(my + b, n_dp)}

    def group(off):
        return {"grp": lax.rem(me + off, n_grp), "dp": my}

    def part(off):
        return {"grp": row_of * inner + lax.rem(lane + off, inner), "dp": my}

    loads = [
        pltpu.make_async_copy(src, dst, in_sem.at[k])
        for k, (src, dst) in enumerate((
            (pre_hbm, pre_ref), (kvb_hbm, kvb_ref), (qb_hbm, qb_ref), (kv_hbm, kv_s), (q_hbm, q_s), (g_hbm, g_s)))
    ]
    for item in loads[:2]:
        item.start()
    barrier = pltpu.get_barrier_semaphore()
    for off in range(1, n_grp):
        pl.semaphore_signal(barrier, inc=1, device_id=group(off), device_id_type=MESH)
    far = [at(a, b) for a, b in across if b > 0]
    for peer in far:
        pl.semaphore_signal(barrier, inc=1, device_id=peer, device_id_type=MESH)
    for item in loads[2:]:
        item.start()

    loads[0].wait()
    loads[1].wait()
    kvb = kvb_ref[...].reshape(1, 2 * WIDTH)
    mine = (pre_ref[...].astype(F32) + kvb).astype(BF16)
    for j in range(KVH):
        pre_all[j // STEP, me, :, (j % STEP) * 2 * HD:(j % STEP + 1) * 2 * HD] = jnp.concatenate(
            [mine[:, j * HD:(j + 1) * HD], mine[:, WIDTH + j * HD:WIDTH + (j + 1) * HD]], axis=1)

    def send(src, dst, sems, recv, peer):
        pltpu.make_async_remote_copy(
            src_ref=src, dst_ref=dst, send_sem=sems.at[0], recv_sem=sems.at[recv],
            device_id=peer, device_id_type=MESH).start()

    def take(like, sem):
        pltpu.make_async_copy(like, like, sem).wait()

    pl.semaphore_wait(barrier, n_grp - 1 + len(far))
    for c in range(KVH // STEP):
        for off in range(1, n_grp):
            send(pre_all.at[c, me], pre_all.at[c, me], ag_sem, 1 + c, group(off))

    length = len_ref[0, 0]
    live_in = lax.broadcasted_iota(jnp.int32, (slots, GCOLS), 0) < length
    live_out = lax.broadcasted_iota(jnp.int32, (slots, HD), 0) < length
    key_at = lax.broadcasted_iota(jnp.int32, (slots, slots), 0)
    row_at = lax.broadcasted_iota(jnp.int32, (slots, slots), 1)
    allow = jnp.concatenate([key_at <= row_at] * GROUP, axis=1)
    pick = (lax.broadcasted_iota(jnp.int32, (GROUP * slots, HD), 1)
            == lax.div(lax.broadcasted_iota(jnp.int32, (GROUP * slots, HD), 0), slots)).astype(F32).astype(BF16)
    bias_row = lax.broadcasted_iota(jnp.int32, (TILE, HD), 0)

    for item in loads[2:]:
        item.wait()
    kv2[...] = (kv_s[...].astype(F32) + kvb).astype(BF16)
    qb = qb_ref[...].reshape(1, QH * HD)
    def ready(j):
        cols = slice(j * GCOLS, (j + 1) * GCOLS)
        qj = heads_down((q_s[:, cols].astype(F32) + qb[:, cols]).astype(BF16))
        gj = g_s[:, cols]
        gj = heads_down(jnp.where(live_in, gj, jnp.zeros_like(gj)))
        q2[j] = qj
        g2[j] = gj
        raw = dot(kv2[:, j * HD:(j + 1) * HD], qj, NT) * factor
        raw = jnp.where(allow, raw, NEG_BIG)
        dpo = dot(kv2[:, WIDTH + j * HD:WIDTH + (j + 1) * HD], gj, NT)
        top = jnp.max(raw, 0, keepdims=True)
        e = jnp.exp(raw - top)
        eown[j] = e
        dpown[j] = dpo
        stat[j, 0:1] = top
        stat[j, 1:2] = jnp.sum(e, 0, keepdims=True)
        stat[j, 2:3] = jnp.sum(e * dpo, 0, keepdims=True)
        gsum[j, 0:1] = jnp.sum(gj.astype(F32), 0, keepdims=True)

    for j in range(KVH):
        ready(j)

    def prompt(j):
        both = pre_all[j // STEP, :, :, (j % STEP) * 2 * HD:(j % STEP + 1) * 2 * HD].reshape(pre_rows, 2 * HD)
        return both[:, :HD], both[:, HD:]

    def keys_of(j):
        return jnp.concatenate([prompt(j)[0], kv2[:, j * HD:(j + 1) * HD]], axis=0)

    rows = []
    for j in range(KVH):
        if j % STEP == 0:
            take(pre_all.at[j // STEP, pl.ds(0, n_grp - 1)], ag_sem.at[1 + j // STEP])
        pk, pv = prompt(j)
        qj = q2[j]
        s_p = dot(pk, qj, NT) * factor
        dp_p = dot(pv, g2[j], NT)
        top_o = stat[j, 0:1]
        top = jnp.maximum(jnp.max(s_p, 0, keepdims=True), top_o)
        e_p = jnp.exp(s_p - top)
        shift = jnp.exp(top_o - top)
        inv = 1.0 / (jnp.sum(e_p, 0, keepdims=True) + shift * stat[j, 1:2])
        scale = shift * inv
        p_p = e_p * inv
        p_o = eown[j] * scale
        dp_o = dpown[j]
        row = jnp.sum(p_p * dp_p, 0, keepdims=True) + scale * stat[j, 2:3]
        ds = jnp.concatenate([(p_p * (dp_p - row)).astype(BF16), (p_o * (dp_o - row)).astype(BF16)], axis=0)
        pb_s[j, :pre_rows] = p_p.astype(BF16)
        stat[j, 3:4] = scale
        ds_s[j] = ds
        heads = dot(ds, pick, NN)
        keys_f = keys_of(j).astype(F32)
        over = jnp.sum(ds.astype(F32), 0, keepdims=True)
        over_high = over.astype(BF16).astype(F32)
        over = jnp.concatenate([over_high, over - over_high, jnp.zeros((TILE - 2, GROUP * slots), F32)], axis=0).astype(BF16)
        key_sum = jnp.sum(dot(over, qj, NN), 0, keepdims=True) * factor
        block = jnp.zeros((TILE, HD), F32)
        for h in range(GROUP):
            part_sum = jnp.sum(heads[:, h:h + 1] * keys_f, 0, keepdims=True) * factor
            block = jnp.where(bias_row == h, part_sum, block)
        block = jnp.where(bias_row == GROUP, key_sum, block)
        rows.append(jnp.where(bias_row == GROUP + 1, gsum[j, 0:1], block))
        if j % STEP == STEP - 1:
            c = j // STEP
            b_all[c, slot] = jnp.concatenate(rows, axis=0).astype(BF16)
            rows = []
            for a, b in across:
                send(b_all.at[c, slot], b_all.at[c, slot], b_sem, 1 + c, at(a, b))
    for j in range(KVH):
        vc = slice(WIDTH + j * HD, WIDTH + (j + 1) * HD)
        kc = slice(j * HD, (j + 1) * HD)
        dkr = (dot(ds_s[j], q2[j], NN) * factor).astype(BF16)
        pg[:, :, kc] = dkr[:pre_rows].reshape(n_grp, own_rows, HD)
        dkv_s[:, kc] = dkr[pre_rows:]
        pb_s[j, pre_rows:] = (eown[j] * stat[j, 3:4]).astype(BF16)
        dvr = dot(pb_s[j], g2[j], NN).astype(BF16)
        pg[:, :, vc] = dvr[:pre_rows].reshape(n_grp, own_rows, HD)
        dkv_s[:, vc] = dvr[pre_rows:]
    for off in range(1, n_grp):
        peer = group(off)
        send(pg.at[peer["grp"]], pr.at[me], rs_sem, 1, peer)

    for j in range(KVH):
        dq = dot(ds_s[j], keys_of(j), TN) * factor
        vals = jnp.concatenate([prompt(j)[1], kv2[:, WIDTH + j * HD:WIDTH + (j + 1) * HD]], axis=0)
        out = dot(pb_s[j], vals, TN)
        for h in range(GROUP):
            here = slice((j * GROUP + h) * HD, (j * GROUP + h + 1) * HD)
            dq_s[:, here] = dq[h * slots:(h + 1) * slots].astype(BF16)
            att_s[:, here] = jnp.where(live_out, out[h * slots:(h + 1) * slots], 0.0).astype(BF16)

    for c in range(KVH // STEP):
        take(b_all.at[c, pl.ds(0, n_slots - 1)], b_sem.at[1 + c])
        total = b_all[c, 0].astype(F32)
        for k in range(1, n_slots):
            total = total + b_all[c, k].astype(F32)
        f_all[c, lane] = total
        for off in range(1, inner):
            send(f_all.at[c, lane], f_all.at[c, lane], f_sem, 1 + c, part(off))
    take(pr.at[pl.ds(0, n_grp - 1)], rs_sem.at[1])
    pr[me] = pg[me]
    acc = pr[0].astype(F32)
    for k in range(1, n_grp):
        acc = acc + pr[k].astype(F32)
    dpre_ref[...] = acc.astype(BF16)
    take(pre_all.at[:, pl.ds(0, n_grp - 1)], ag_sem.at[0])
    take(pr.at[pl.ds(0, n_grp - 1)], rs_sem.at[0])
    take(b_all.at[:, pl.ds(0, n_slots - 1)], b_sem.at[0])
    take(f_all.at[:, pl.ds(0, inner - 1)], f_sem.at[0])
    for c in range(KVH // STEP):
        take(f_all.at[c, pl.ds(0, inner - 1)], f_sem.at[1 + c])
        total = f_all[c, 0]
        for k in range(1, inner):
            total = total + f_all[c, k]
        for k in range(STEP):
            j = c * STEP + k
            for h in range(GROUP):
                qsum_ref[pl.ds((j * GROUP + h) * HD, HD)] = total[k * TILE + h]
            kvsum_ref[pl.ds(j * HD, HD)] = total[k * TILE + GROUP]
            kvsum_ref[pl.ds(WIDTH + j * HD, HD)] = total[k * TILE + GROUP + 1]


def write_out(*refs):
    count = (len(refs) - 1) // 2
    copies = [pltpu.make_async_copy(refs[k], refs[count + k], refs[-1].at[k]) for k in range(count)]
    for item in copies:
        item.start()
    for item in copies:
        item.wait()


def local(n_grp, n_dp, query, resp_kv, prefix_kv, query_bias, kv_bias, out_grad, lengths):
    slots = query.shape[1]
    own_rows = prefix_kv.shape[1]
    pre_rows = own_rows * n_grp
    inner = 2 if n_grp % 2 == 0 and n_grp // 2 * n_dp <= DIRECT else n_grp
    n_slots = n_grp // inner * n_dp
    chunks = KVH // STEP
    qw = QH * HD
    kw = 2 * WIDTH
    hbm = pl.BlockSpec(memory_space=pltpu.HBM)
    vmem = pl.BlockSpec(memory_space=pltpu.VMEM)
    dma = lambda *n: pltpu.SemaphoreType.DMA(n)
    shapes = (
        jax.ShapeDtypeStruct((slots, qw), BF16),
        jax.ShapeDtypeStruct((slots, qw), BF16),
        jax.ShapeDtypeStruct((slots, kw), BF16),
        jax.ShapeDtypeStruct((own_rows, kw), BF16),
        jax.ShapeDtypeStruct((qw,), F32),
        jax.ShapeDtypeStruct((kw,), F32),
    )
    outs = pl.pallas_call(
        functools.partial(kernel, n_grp, n_dp, inner),
        name="replay",
        out_shape=shapes,
        in_specs=[pl.BlockSpec(memory_space=pltpu.SMEM)] + [hbm] * 6,
        out_specs=(vmem,) * 6,
        scratch_shapes=[
            pltpu.VMEM((own_rows, kw), BF16),
            pltpu.VMEM((qw,), F32),
            pltpu.VMEM((kw,), F32),
            pltpu.VMEM((slots, qw), BF16),
            pltpu.VMEM((slots, qw), BF16),
            pltpu.VMEM((slots, kw), BF16),
            pltpu.VMEM((KVH, GROUP * slots, HD), BF16),
            pltpu.VMEM((KVH, GROUP * slots, HD), BF16),
            pltpu.VMEM((slots, kw), BF16),
            pltpu.VMEM((KVH, slots, GROUP * slots), F32),
            pltpu.VMEM((KVH, slots, GROUP * slots), F32),
            pltpu.VMEM((KVH, TILE, GROUP * slots), F32),
            pltpu.VMEM((KVH, TILE, HD), F32),
            pltpu.VMEM((KVH, pre_rows + slots, GROUP * slots), BF16),
            pltpu.VMEM((KVH, pre_rows + slots, GROUP * slots), BF16),
            pltpu.VMEM((chunks, n_grp, own_rows, STEP * 2 * HD), BF16),
            pltpu.VMEM((n_grp, own_rows, kw), BF16),
            pltpu.VMEM((n_grp, own_rows, kw), BF16),
            pltpu.VMEM((chunks, n_slots, STEP * TILE, HD), BF16),
            pltpu.VMEM((chunks, inner, STEP * TILE, HD), F32),
            dma(6), dma(1 + chunks), dma(2), dma(1 + chunks), dma(1 + chunks),
        ],
        compiler_params=pltpu.CompilerParams(
            collective_id=0, has_side_effects=True, vmem_limit_bytes=24 * 1024 * 1024
        ),
    )(lengths, *(pltpu.with_memory_space_constraint(x, pltpu.HBM) for x in (query[0], resp_kv[0], prefix_kv[0], query_bias, kv_bias, out_grad[0])))
    att, dq, dkv, dpre, qsum, kvsum = pl.pallas_call(
        write_out,
        name="write_out",
        out_shape=shapes,
        in_specs=[vmem] * 6,
        out_specs=(hbm,) * 6,
        scratch_shapes=[dma(6)],
        compiler_params=pltpu.CompilerParams(vmem_limit_bytes=1024 * 1024),
    )(*outs)
    return att[None], dq[None], dkv[None], dpre[None], qsum, kvsum


def solution(mesh):
    return jax.shard_map(
        functools.partial(local, mesh.shape["grp"], mesh.shape["dp"]),
        mesh=mesh,
        in_specs=(
            P("dp", "grp", None),
            P("dp", "grp", None),
            P("dp", "grp", None),
            P(),
            P(),
            P("dp", "grp", None),
            P("dp", "grp"),
        ),
        out_specs=(
            P("dp", "grp", None),
            P("dp", "grp", None),
            P("dp", "grp", None),
            P("dp", "grp", None),
            P(),
            P(),
        ),
        check_vma=False,
    )
```
